32 devices in a mesh: groups: 2 (over y), hx: 16 (over z, x, core).
Axes of the slice: x: 2, y: 2, z: 4, core: 2. Of those that a mesh axis runs over, the one named last changes fastest.
Arguments:
- tokens: bfloat16 [32, 8192], P(('groups', 'hx')), parts along dimension 0, may hold values from -6 to 6
- gate_codes: bfloat16 [8192, 26624], P(None, 'hx'), may hold values from -8 to 7, as said below
- gate_scales: float32 [64, 26624], P(None, 'hx'), may hold values from 0.00077339803 to 0.00773398
- up_codes: bfloat16 [8192, 26624], P(None, 'hx'), may hold values from -8 to 7, as said below
- up_scales: float32 [64, 26624], P(None, 'hx'), may hold values from 0.00077339803 to 0.00773398
- down_codes: bfloat16 [26624, 8192], P('hx'), may hold values from -8 to 7, as said below
- down_scales: float32 [8192], replicated, may hold values from 0.00061286293 to 0.006128629
- hadamard: int32 [52, 52], replicated, may hold values from -1 to 1, as said below
Outputs:
- mixed: bfloat16 [32, 8192], P(('groups', 'hx')), parts along dimension 0
The draws below stay inside these ranges and needn't reach their ends.
There are 2 independent parts, one for each index of `groups`. The reference program is written for one: setup_inputs(seed, part) draws one part's arguments, and reference() takes and returns one part's arrays. A program takes and returns all parts, laid end to end along the dimension named above; an argument that names none is the same for every part. Nothing has to cross between parts.
Inputs may be any that keep to these rules, and one draw needn't show every extreme that they name: `gate_codes`: whole numbers. `up_codes`: whole numbers. `down_codes`: whole numbers. `hadamard`: a Hadamard matrix: every entry is -1 or 1 and any two rows are orthogonal.
All inputs are finite; a program needn't handle non-finite values.
Results may differ from the reference program's by a relative error of at most 0.015.
Values may be sent and summed in bfloat16 or wider, within the bound.
A program may use at most 192 MiB of HBM per device.

```python
import math
import jax
import jax.numpy as jnp
import numpy as np
from jax import lax

D = 8192
HA = 512
HB = 52
GROUP = 128
FF = 26624
TOKENS = 16


def field_product(left, right):
    return ((left[0] * right[0] + 2 * left[1] * right[1]) % 5, (left[0] * right[1] + left[1] * right[0]) % 5)


def paley_table():
    members = [(first, second) for first in range(5) for second in range(5)]
    squares = set()
    for member in members:
        if member != (0, 0):
            squares.add(field_product(member, member))
    count = len(members)
    conference = np.zeros((count + 1, count + 1), dtype=np.int64)
    conference[0, 1:] = 1
    conference[1:, 0] = 1
    for row_pos in range(count):
        for col_pos in range(count):
            differ = ((members[row_pos][0] - members[col_pos][0]) % 5, (members[row_pos][1] - members[col_pos][1]) % 5)
            if differ == (0, 0):
                conference[row_pos + 1, col_pos + 1] = 0
            elif differ in squares:
                conference[row_pos + 1, col_pos + 1] = 1
            else:
                conference[row_pos + 1, col_pos + 1] = -1
    plus_block = np.array([[1, 1], [1, -1]], dtype=np.int64)
    zero_block = np.array([[1, -1], [-1, -1]], dtype=np.int64)
    return np.kron(conference, plus_block) + np.kron(np.eye(count + 1, dtype=np.int64), zero_block)


def draw_codes(key, rows_total, cols_total):
    values = jax.random.randint(key, (rows_total, cols_total), -8, 8, dtype=jnp.int32)
    return values.astype(jnp.float32).astype(jnp.bfloat16)


def draw_gate_codes(key, part):
    return draw_codes(jax.random.fold_in(key, 11), D, FF)


def draw_up_codes(key, part):
    return draw_codes(jax.random.fold_in(key, 12), D, FF)


def draw_down_codes(key, part):
    return draw_codes(jax.random.fold_in(key, 13), FF, D)


def draw_hadamard(key, part):
    base = jnp.asarray(paley_table().astype(np.int32))
    row_order = jax.random.permutation(jax.random.fold_in(key, 21), HB)
    col_order = jax.random.permutation(jax.random.fold_in(key, 22), HB)
    row_signs = 2 * jax.random.randint(jax.random.fold_in(key, 23), (HB,), 0, 2, dtype=jnp.int32) - 1
    col_signs = 2 * jax.random.randint(jax.random.fold_in(key, 24), (HB,), 0, 2, dtype=jnp.int32) - 1
    table = base[row_order][:, col_order]
    return (table * row_signs[:, None] * col_signs[None, :]).astype(jnp.int32)


def levels(own_key, extent, pieces, least, top_value):
    loudness = 1.0
    for axis_at, blocks in pieces:
        steps = jax.random.uniform(jax.random.fold_in(jax.random.fold_in(own_key, 6), axis_at), (blocks,), jnp.float32, least / len(pieces), top_value / len(pieces))
        loudness = loudness * jnp.repeat(jnp.exp(steps), extent[axis_at] // blocks).reshape((-1,) + (1,) * (len(extent) - 1 - axis_at))
    return loudness


def gaussian(rng, extent, width, bound, shards=(), kind=jnp.bfloat16):
    result = jax.random.normal(rng, extent, jnp.float32) * width
    if len(shards) > 0:
        result = levels(rng, extent, shards, -0.22, 0.18) * result
    return jnp.clip(result, min=-bound, max=bound).astype(kind)


def setup_inputs(seed: int = 0, part: int = 0) -> dict:
    seeds = jax.random.split(jax.random.key(seed), 9)
    part_splits = jax.random.split(jax.random.fold_in(seeds[8], part), 9)
    tokens = gaussian(part_splits[0], (TOKENS, D), 1.0, 6.0, ((0, 16),))
    gate_codes = draw_gate_codes(jax.random.fold_in(seeds[8], 71), part)
    gate_scales = jnp.clip(jnp.exp(math.log(0.00773398) - 2.3025851 * jax.random.uniform(seeds[2], (D // GROUP, FF), jnp.float32) ** levels(seeds[2], (D // GROUP, FF), ((1, 16),), -0.2, 0.2)), 0.00077339803, 0.00773398)
    up_codes = draw_up_codes(jax.random.fold_in(seeds[8], 71), part)
    up_scales = jnp.clip(jnp.exp(math.log(0.00773398) - 2.3025851 * jax.random.uniform(seeds[4], (D // GROUP, FF), jnp.float32) ** levels(seeds[4], (D // GROUP, FF), ((1, 16),), -0.2, 0.2)), 0.00077339803, 0.00773398)
    down_codes = draw_down_codes(jax.random.fold_in(seeds[8], 71), part)
    down_scales = jnp.clip(jnp.exp(jax.random.uniform(seeds[6], (D,), jnp.float32, math.log(0.00061286293), math.log(0.006128629))), 0.00061286293, 0.006128629)
    hadamard = draw_hadamard(jax.random.fold_in(seeds[8], 71), part)
    return {"tokens": tokens, "gate_codes": gate_codes, "gate_scales": gate_scales, "up_codes": up_codes, "up_scales": up_scales, "down_codes": down_codes, "down_scales": down_scales, "hadamard": hadamard}


def sylvester(size):
    index_vec = jnp.arange(size, dtype=jnp.int32)
    parity = jnp.zeros((size, size), jnp.int32)
    for level in range(max(size.bit_length() - 1, 0)):
        left_bits = jnp.right_shift(index_vec[:, None], level) & 1
        right_bits = jnp.right_shift(index_vec[None, :], level) & 1
        parity = parity + left_bits * right_bits
    return (1 - 2 * (parity % 2)).astype(jnp.float32)

def dequantize(codes, scales):
    row_total, col_total = codes.shape
    group_total = scales.shape[0]
    grouped = codes.astype(jnp.float32).reshape(group_total, row_total // group_total, col_total)
    return (grouped * scales[:, None, :]).reshape(row_total, col_total).astype(jnp.bfloat16)

def reference(tokens, gate_codes, gate_scales, up_codes, up_scales, down_codes, down_scales, hadamard):
    gate_weight = dequantize(gate_codes, gate_scales)
    gate = jnp.dot(tokens, gate_weight, preferred_element_type=jnp.float32)
    up_weight = dequantize(up_codes, up_scales)
    up_part = jnp.dot(tokens, up_weight, preferred_element_type=jnp.float32)
    hidden = jax.nn.silu(gate) * up_part
    cube = hidden.reshape(TOKENS, HA, HB)
    cube = jnp.einsum('tab,ac->tcb', cube, sylvester(HA), precision=lax.Precision.HIGHEST)
    cube = jnp.einsum('tcb,bd->tcd', cube, hadamard.astype(jnp.float32), precision=lax.Precision.HIGHEST)
    rotated = (cube.reshape(TOKENS, FF) * (1.0 / math.sqrt(FF))).astype(jnp.bfloat16)
    summed = jnp.dot(rotated, down_codes, preferred_element_type=jnp.float32)
    return (summed * down_scales[None, :]).astype(jnp.bfloat16)
```

```python
import functools
import math

import jax
import jax.numpy as jnp
from jax import lax
from jax.experimental import pallas as pl
from jax.experimental.pallas import tpu as pltpu
from jax.sharding import PartitionSpec as P

HA = 512
HB = 52
FF = 26624


def sylvester(size):
    index_vec = jnp.arange(size, dtype=jnp.int32)
    parity = jnp.zeros((size, size), jnp.int32)
    for level in range(max(size.bit_length() - 1, 0)):
        left_bits = jnp.right_shift(index_vec[:, None], level) & 1
        right_bits = jnp.right_shift(index_vec[None, :], level) & 1
        parity = parity + left_bits * right_bits
    return (1 - 2 * (parity % 2)).astype(jnp.float32)


def dequantize(codes, scales):
    row_total, col_total = codes.shape
    group_total = scales.shape[0]
    grouped = codes.astype(jnp.float32).reshape(group_total, row_total // group_total, col_total)
    return (grouped * scales[:, None, :]).reshape(row_total, col_total).astype(jnp.bfloat16)


LANES = 128
WIDE = 2 * LANES
PIECES = 4
CHUNK = 512
SLOTS = 6
DOWN_COLS = 1024
DOWN_SLOTS = 3
BLOCK = 64
OUT_ROWS = 16


def kernel(
    n, groups, tok_ref, gate_ref, gscale_ref, up_ref, uscale_ref, down_ref, dscale_ref, had_ref,
    out_ref,
    ring, weights, dring, down, gs, us, ds, had, corner, table, local, tok_row, tok_f32, tok_out, tok, stage, lhs, acc,
    xsend, xrecv, zbuf, recv_z, rbuf, rot, part, pair_out, pair_in, sums, recv_c,
    ring_sem, load_sem, down_sem, tok_ssem, tok_rsem, fwd_ssem, fwd_rsem, x_ssem, x_rsem, z_ssem, z_rsem, r_ssem, r_rsem,
    p_ssem, p_rsem, c_ssem, c_rsem,
):
    f32, bf16, f8 = jnp.float32, jnp.bfloat16, jnp.float8_e4m3fn
    mine = lax.axis_index("groups")
    me = lax.axis_index("hx")
    chips = n // 2
    chip, core = lax.div(me, 2), lax.rem(me, 2)
    units = gate_ref.shape[1]
    tiles = units // LANES
    half_rows = gate_ref.shape[0] // groups
    chunks = half_rows // CHUNK
    piece_rows = tok.shape[3]
    down_chunks = down.shape[0]
    other = lax.rem(mine + 1, groups)

    def device(group, index):
        return {"groups": group, "hx": index}

    def remote(src, dst, send_sem, recv_sem, peer):
        return pltpu.make_async_remote_copy(
            src_ref=src, dst_ref=dst, send_sem=send_sem, recv_sem=recv_sem,
            device_id=peer, device_id_type=pl.DeviceIdType.MESH,
        )

    def chip_at(step):
        return lax.rem(chip + step, chips)

    partner = device(mine, chip * 2 + 1 - core)
    peers = [device(mine, lax.rem(me + step, n)) for step in range(1, n)]
    across = [device(other, chip_at(step) * 2 + core) for step in range(chips)]

    def weight_copies(c):
        rows = pl.ds(pl.multiple_of(mine * half_rows + c * CHUNK, CHUNK), CHUNK)
        slot = c % SLOTS
        return [
            pltpu.make_async_copy(src.at[rows], ring.at[slot, w], ring_sem.at[slot, w])
            for w, src in enumerate((gate_ref, up_ref))
        ]

    def down_copy(c):
        cols = pl.ds(c * DOWN_COLS, DOWN_COLS)
        return pltpu.make_async_copy(down_ref.at[:, cols], dring.at[c % DOWN_SLOTS], down_sem.at[c % DOWN_SLOTS])

    scale_rows = gs.shape[0]
    half_scales = pl.ds(pl.multiple_of(mine * scale_rows, scale_rows), scale_rows)
    loads = [
        pltpu.make_async_copy(src, dst, load_sem.at[i])
        for i, (src, dst) in enumerate(
            (
                (tok_ref, tok_row), (had_ref, had), (dscale_ref, ds),
                (gscale_ref.at[half_scales], gs), (uscale_ref.at[half_scales], us),
            )
        )
    ]

    barrier = pltpu.get_barrier_semaphore()
    for peer in peers + across:
        pl.semaphore_signal(barrier, inc=1, device_id=peer, device_id_type=pl.DeviceIdType.MESH)
    for copy in loads:
        copy.start()
    for c in range(SLOTS):
        for copy in weight_copies(c):
            copy.start()
    loads[0].wait()
    row = tok_row[...].astype(f32)
    for k in range(tok_f32.shape[0]):
        tok_f32[k : k + 1, :] = row[:, k * LANES : (k + 1) * LANES]
    for h in range(groups):
        for p in range(PIECES):
            start = (h * PIECES + p) * piece_rows
            tok_out[h, p] = tok_f32[start : start + piece_rows, :].astype(bf16)
    for p in range(PIECES):
        tok[p, core, chip] = tok_out[mine, p]
    loads[1].wait()

    half = LANES // 2
    hb = had.shape[0]
    ha = units // hb
    corner[...] = jnp.zeros_like(corner)
    corner[:hb, :hb] = had[...].astype(f32)
    left_bits = lax.broadcasted_iota(jnp.int32, (ha, ha), 0) & lax.broadcasted_iota(jnp.int32, (ha, ha), 1)
    parity = jnp.zeros((ha, ha), jnp.int32)
    for level in range(ha.bit_length() - 1):
        parity = parity ^ (jnp.right_shift(left_bits, level) & 1)
    corner[half : half + ha, half : half + ha] = (1 - 2 * parity).astype(f32)

    def digits(unit):
        high = jnp.floor((unit + 0.5) * (1.0 / hb))
        return high, unit - hb * high

    def wide(i, carry):
        shape = (LANES, LANES)
        unit = (lax.broadcasted_iota(jnp.int32, shape, 1) + i * LANES).astype(f32)
        at = lax.broadcasted_iota(jnp.int32, shape, 0).astype(f32)
        high, low = digits(unit)
        pick = jnp.where((at == low) | (at == high + half), 1.0, 0.0).astype(bf16)
        table[i] = jnp.dot(corner[...].astype(bf16), pick, preferred_element_type=f32).astype(bf16)
        return carry

    lax.fori_loop(0, tiles, wide, 0)
    factors = jnp.concatenate([table[j] for j in range(tiles)], axis=1)

    def build(i, carry):
        shape = (LANES, LANES)
        unit = (lax.broadcasted_iota(jnp.int32, shape, 0) + i * LANES).astype(f32)
        at = lax.broadcasted_iota(jnp.int32, shape, 1).astype(f32)
        high, low = digits(unit)
        pick = jnp.concatenate(
            [jnp.where(at == low, 1.0, 0.0), jnp.where(at == high + half, 1.0, 0.0)], axis=0
        ).astype(bf16)
        both = jnp.dot(pick, factors, preferred_element_type=f32)
        rows = pl.ds(pl.multiple_of(i * LANES, LANES), LANES)
        local[rows, :] = (both[:LANES] * both[LANES:]).astype(f8)
        return carry

    lax.fori_loop(0, tiles // 2, build, 0)

    pl.semaphore_wait(barrier, len(peers) + len(across))

    hops = [(d, step) for d in range(groups) for step in range(chips) if (d, step) != (0, 0)]

    def tok_send(p, d, step):
        group = lax.rem(mine + d, groups)
        return remote(
            tok_out.at[group, p], tok.at[p, core, d * chips + chip], tok_ssem.at[p, d * chips + step],
            tok_rsem.at[p, d * chips + chip], device(group, chip_at(step) * 2 + core),
        )

    def tok_arrive(p, d, step):
        source = d * chips + chip_at(step)
        return remote(
            tok_out.at[0, p], tok.at[p, core, source], tok_ssem.at[p, d * chips + step], tok_rsem.at[p, source],
            device(lax.rem(mine + d, groups), chip_at(step) * 2 + core),
        )

    def forward(p, which):
        return remote(tok.at[p, which], tok.at[p, which], fwd_ssem.at[p], fwd_rsem.at[p], partner)

    for p in range(PIECES):
        for d, step in hops:
            tok_send(p, d, step).start()

    lhs[...] = jnp.zeros_like(lhs)
    acc[...] = jnp.zeros_like(acc)
    lax.fori_loop(tiles // 2, tiles, build, 0)

    def convert(c):
        for copy in weight_copies(c):
            copy.wait()

        def block(k, carry):
            rows = pl.ds(pl.multiple_of(k * BLOCK, BLOCK), BLOCK)
            to = pl.ds(pl.multiple_of(c * CHUNK + k * BLOCK, BLOCK), BLOCK)
            for w in range(2):
                weights[w, to, :] = ring[c % SLOTS, w, rows, :].astype(f8)
            return carry

        lax.fori_loop(0, CHUNK // BLOCK, block, 0)
        if c + SLOTS < chunks:
            for copy in weight_copies(c + SLOTS):
                copy.start()
        elif c + SLOTS - chunks < DOWN_SLOTS:
            down_copy(c + SLOTS - chunks).start()

    def convert_down(c):
        down_copy(c).wait()

        def block(k, carry):
            rows = pl.ds(pl.multiple_of(k * BLOCK, BLOCK), BLOCK)
            down[c, rows, :] = dring[c % DOWN_SLOTS, rows, :].astype(f8)
            return carry

        lax.fori_loop(0, units // BLOCK, block, 0)
        if c + DOWN_SLOTS < down_chunks:
            down_copy(c + DOWN_SLOTS).start()

    def relay(p):
        for d, step in hops:
            tok_arrive(p, d, step).wait_recv()
        forward(p, core).start()

    def ready(p):
        forward(p, 1 - core).wait_recv()
        stage[...] = tok[p].reshape(stage.shape).astype(f32)
        for k in range(piece_rows):
            part_rows = [
                stage[pl.ds(w * n * piece_rows + k, n, stride=piece_rows), :] for w in range(2)
            ]
            both = jnp.concatenate(
                [part_rows[0][:chips], part_rows[1][:chips], part_rows[0][chips:], part_rows[1][chips:]], axis=0
            ).astype(bf16)
            q, odd = divmod(k, 2)
            lhs[q, odd * 2 * n : (odd + 1) * 2 * n, odd * LANES : (odd + 1) * LANES] = both

    def products(p, cols, tail):
        sums_now = [None, None]
        for q in range(piece_rows // 2):
            left = lhs[q]
            row = p * piece_rows + 2 * q
            rows = slice(row * LANES, (row + 2) * LANES)
            if tail:
                right = jnp.concatenate([weights[0, rows, cols], weights[1, rows, cols]], axis=1)
                scale = jnp.concatenate([gs[row : row + 2, cols], us[row : row + 2, cols]], axis=1)
                sides = [(right, scale)]
            else:
                sides = [(weights[w, rows, cols], scale[row : row + 2, cols]) for w, scale in ((0, gs), (1, us))]
            for w, (right, scale) in enumerate(sides):
                res = jnp.dot(left, right, preferred_element_type=f32)
                new = res[: 2 * n] * scale[0:1, :] + res[2 * n :] * scale[1:2, :]
                sums_now[w] = new if sums_now[w] is None else sums_now[w] + new
        if tail:
            width = sums_now[0].shape[1] // 2
            return sums_now[0][:, :width], sums_now[0][:, width:]
        return sums_now

    spans = [(at, min(WIDE, units - at)) for at in range(0, units, WIDE)]

    def x_send(j, width):
        at = (j, slice(None), slice(None), pl.ds(0, width))
        return remote(xsend.at[at], xrecv.at[at], x_ssem.at[j], x_rsem.at[j], across[0])

    def run(p):
        for j, (at, width) in enumerate(spans):
            cols = slice(at, at + width)
            pair = products(p, cols, width < WIDE)
            for w in range(2):
                if p + 1 < PIECES:
                    acc[w, :, cols] += pair[w]
                else:
                    total = acc[w, :, cols] + pair[w]
                    acc[w, :n, cols] = total[:n]
                    xsend[j, w, :, :width] = total[n:].astype(bf16)
            if p + 1 == PIECES:
                x_send(j, width).start()

    for copy in loads[2:]:
        copy.wait()
    early = chunks - 2
    for c in range(early):
        convert(c)
    relay(0)
    convert(early)
    relay(1)
    convert(early + 1)
    for p in range(PIECES):
        ready(p)
        run(p)
        if p + 2 < PIECES:
            relay(p + 2)

    for c in range(2):
        convert_down(c)
    turned = None
    for j, (at, width) in enumerate(spans):
        x_send(j, width).wait_recv()
        cols = slice(at, at + width)
        gate = acc[0, :n, cols] + xrecv[j, 0, :, :width].astype(f32)
        lift = acc[1, :n, cols] + xrecv[j, 1, :, :width].astype(f32)
        hidden = (gate / (1.0 + jnp.exp(-gate)) * lift).astype(bf16)
        new = jnp.dot(hidden, local[cols, :], preferred_element_type=f32)
        turned = new if turned is None else turned + new
    turned = turned.astype(bf16)

    owners = zbuf.shape[0]
    quarter = n // 4

    def owner_at(o):
        return quarter + (o % 2) * quarter + o // 2

    def held(o):
        return len(range(o, tiles, owners))

    for j in range(tiles):
        zbuf[j % owners, j // owners] = turned[:, j * LANES : (j + 1) * LANES]

    def z_out(o):
        count = pl.ds(0, held(o))
        return remote(
            zbuf.at[o, count], recv_z.at[me, count], z_ssem.at[o], z_rsem.at[me], device(mine, owner_at(o))
        )

    for o in range(owners):

        @pl.when(me != owner_at(o))
        def _():
            z_out(o).start()

        @pl.when(me == owner_at(o))
        def _():
            recv_z[me] = zbuf[o]

    for c in range(2, 5):
        convert_down(c)

    place = me - quarter
    number = lax.rem(place, quarter) * 2 + lax.div(place, quarter)
    owns = jnp.logical_and(me >= quarter, me < 3 * quarter)
    extra = tiles % owners
    scale = 1.0 / math.sqrt(units * n)

    def r_out(i, count):
        at = pl.ds(0, count)
        peer = lax.rem(me + i, n)
        return remote(rbuf.at[peer, at], rot.at[number, at], r_ssem.at[i - 1], r_rsem.at[number], device(mine, peer))

    def turn(count):
        at = pl.ds(0, count)
        for i in range(1, n):
            peer = lax.rem(me + i, n)
            remote(
                zbuf.at[0, at], recv_z.at[peer, at], z_ssem.at[0], z_rsem.at[peer], device(mine, peer)
            ).wait_recv()
        for t in range(count):
            cube = [recv_z[h, t].astype(f32) for h in range(n)]
            span = 1
            while span < n:
                nxt = list(cube)
                for h in range(n):
                    if h & span == 0:
                        nxt[h] = cube[h] + cube[h | span]
                        nxt[h | span] = cube[h] - cube[h | span]
                cube = nxt
                span *= 2
            for h in range(n):
                rbuf[h, t] = (cube[h] * scale).astype(bf16)
        for i in range(1, n):
            r_out(i, count).start()
        rot[number] = rbuf[me]

    many, few = held(0), held(owners - 1)

    def by_count(action):
        if extra == 0:
            pl.when(owns)(lambda: action(many))
        else:
            pl.when(jnp.logical_and(owns, number < extra))(lambda: action(many))
            pl.when(jnp.logical_and(owns, number >= extra))(lambda: action(few))

    by_count(turn)

    for c in range(5, down_chunks):
        convert_down(c)

    for o in range(owners):

        @pl.when(me != owner_at(o))
        def _():
            count = pl.ds(0, held(o))
            remote(
                rbuf.at[0, count], rot.at[o, count], r_ssem.at[0], r_rsem.at[o], device(mine, owner_at(o))
            ).wait_recv()

    rotated = jnp.concatenate([rot[j % owners, j // owners] for j in range(tiles)], axis=1)

    out_pieces = recv_c.shape[0]
    per_piece = down_chunks // out_pieces
    blocks = DOWN_COLS // LANES
    own_rows = chips * OUT_ROWS

    def pair_copy(p, which):
        at = pl.ds(which * chips, chips)
        return remote(pair_out.at[p, at], pair_in.at[p], p_ssem.at[p], p_rsem.at[p], partner)

    def c_out(p, step):
        to = chip_at(step)
        return remote(
            sums.at[p, to], recv_c.at[p, chip], c_ssem.at[p, step - 1], c_rsem.at[p, chip], device(mine, to * 2 + core)
        )

    def c_in(p, step):
        source = chip_at(step)
        return remote(
            sums.at[p, source], recv_c.at[p, source], c_ssem.at[p, step - 1], c_rsem.at[p, source],
            device(mine, source * 2 + core),
        )

    def finish(p):
        pair_copy(p, core).wait_recv()
        rows = pl.ds(pl.multiple_of(core * own_rows, own_rows), own_rows)
        both = part[p, rows, :] + pair_in[p].reshape(own_rows, LANES).astype(f32)
        sums[p] = both.astype(bf16).reshape(chips, OUT_ROWS, LANES)
        for step in range(1, chips):
            c_out(p, step).start()
        recv_c[p, chip] = sums[p, chip]

    for p in range(out_pieces):
        for k in range(per_piece):
            res = jnp.dot(rotated, down[p * per_piece + k], preferred_element_type=f32)
            for b in range(blocks):
                part[p, pl.ds(k * blocks + b, n, stride=OUT_ROWS), :] = res[:, b * LANES : (b + 1) * LANES]
        pair_out[p] = part[p].astype(bf16).reshape(n, OUT_ROWS, LANES)
        pair_copy(p, 1 - core).start()
        if p > 0:
            finish(p - 1)
    finish(out_pieces - 1)

    for p in range(out_pieces):
        for step in range(1, chips):
            c_in(p, step).wait_recv()
        total = recv_c[p, 0].astype(f32)
        for h in range(1, chips):
            total = total + recv_c[p, h].astype(f32)
        for r in range(OUT_ROWS):
            cols = slice((p * OUT_ROWS + r) * LANES, (p * OUT_ROWS + r + 1) * LANES)
            out_ref[:, cols] = (total[r : r + 1, :] * ds[:, cols]).astype(out_ref.dtype)

    for p in range(PIECES):
        for d, step in hops:
            tok_send(p, d, step).wait_send()
        forward(p, core).wait_send()
    for j, (at, width) in enumerate(spans):
        x_send(j, width).wait_send()
    for o in range(owners):

        @pl.when(me != owner_at(o))
        def _():
            z_out(o).wait_send()

    def drain(count):
        for i in range(1, n):
            r_out(i, count).wait_send()

    by_count(drain)
    for p in range(out_pieces):
        pair_copy(p, 1 - core).wait_send()
        for step in range(1, chips):
            c_out(p, step).wait_send()


def fused(n, groups, tokens, gate_codes, gate_scales, up_codes, up_scales, down_codes, down_scales, hadamard):
    depth, units = gate_codes.shape
    width = down_codes.shape[1]
    tiles = units // LANES
    piece_rows = depth // (groups * PIECES * LANES)
    half_scales = (gate_scales.shape[0] // groups, units)
    out_pieces = width // (LANES * OUT_ROWS)
    owners = n // 2
    held = -(-tiles // owners)
    spans = -(-units // WIDE)
    chips = n // 2
    bf16, f32, f8 = jnp.bfloat16, jnp.float32, jnp.float8_e4m3fn
    dma = pltpu.SemaphoreType.DMA
    vmem = pltpu.VMEM
    return pl.pallas_call(
        functools.partial(kernel, n, groups),
        out_shape=jax.ShapeDtypeStruct((1, width), bf16),
        in_specs=[pl.BlockSpec(memory_space=pl.ANY)] * 8,
        out_specs=pl.BlockSpec(memory_space=pltpu.VMEM),
        scratch_shapes=[
            vmem((SLOTS, 2, CHUNK, units), bf16),
            vmem((2, depth // groups, units), f8),
            vmem((DOWN_SLOTS, units, DOWN_COLS), bf16),
            vmem((width // DOWN_COLS, units, DOWN_COLS), f8),
            vmem(half_scales, f32),
            vmem(half_scales, f32),
            vmem((1, width), f32),
            vmem(hadamard.shape, hadamard.dtype),
            vmem((LANES, LANES), f32),
            vmem((tiles, LANES, LANES), bf16),
            vmem((units, units), f8),
            vmem((1, depth), bf16),
            vmem((depth // LANES, LANES), f32),
            vmem((groups, PIECES, piece_rows, LANES), bf16),
            vmem((PIECES, 2, n, piece_rows, LANES), bf16),
            vmem((2 * n * piece_rows, LANES), f32),
            vmem((piece_rows // 2, 4 * n, WIDE), bf16),
            vmem((2, 2 * n, units), f32),
            vmem((spans, 2, n, WIDE), bf16),
            vmem((spans, 2, n, WIDE), bf16),
            vmem((owners, held, n, LANES), bf16),
            vmem((n, held, n, LANES), bf16),
            vmem((n, held, n, LANES), bf16),
            vmem((owners, held, n, LANES), bf16),
            vmem((out_pieces, n * OUT_ROWS, LANES), f32),
            vmem((out_pieces, n, OUT_ROWS, LANES), bf16),
            vmem((out_pieces, chips, OUT_ROWS, LANES), bf16),
            vmem((out_pieces, chips, OUT_ROWS, LANES), bf16),
            vmem((out_pieces, chips, OUT_ROWS, LANES), bf16),
            dma((SLOTS, 2)),
            dma((5,)),
            dma((DOWN_SLOTS,)),
            dma((PIECES, n)),
            dma((PIECES, n)),
            dma((PIECES,)),
            dma((PIECES,)),
            dma((spans,)),
            dma((spans,)),
            dma((owners,)),
            dma((n,)),
            dma((n - 1,)),
            dma((owners,)),
            dma((out_pieces,)),
            dma((out_pieces,)),
            dma((out_pieces, chips - 1)),
            dma((out_pieces, chips)),
        ],
        compiler_params=pltpu.CompilerParams(
            collective_id=0, has_side_effects=True, vmem_limit_bytes=67043328
        ),
    )(
        tokens, gate_codes, gate_scales, up_codes, up_scales, down_codes, down_scales.reshape(1, width), hadamard,
    )


def fits(n, groups, tokens, gate_scales, down_codes):
    rows, depth = tokens.shape
    units, width = down_codes.shape
    scale_rows = gate_scales.shape[0]
    return (
        rows == 1
        and n == 16
        and groups == 2
        and HA % n == 0
        and units * n == HA * HB
        and HA // n <= LANES // 2
        and HB <= LANES // 2
        and depth == scale_rows * LANES
        and scale_rows % (groups * PIECES * 8) == 0
        and depth == 8 * groups * CHUNK
        and width == 8 * DOWN_COLS
        and units % LANES == 0
        and n // 2 <= units // LANES <= n
    )


def per_device(
    tokens, gate_codes, gate_scales, up_codes, up_scales, down_codes, down_scales, hadamard
):
    n = lax.axis_size("hx")
    groups = lax.axis_size("groups")
    if fits(n, groups, tokens, gate_scales, down_codes):
        return fused(
            n, groups, tokens, gate_codes, gate_scales, up_codes, up_scales, down_codes, down_scales, hadamard
        )
    gate_weight = dequantize(gate_codes, gate_scales)
    up_weight = dequantize(up_codes, up_scales)
    tile_rows = lax.all_gather(tokens, "hx", axis=0, tiled=True)
    gate = jnp.dot(tile_rows, gate_weight, preferred_element_type=jnp.float32)
    up_part = jnp.dot(tile_rows, up_weight, preferred_element_type=jnp.float32)
    hidden = jax.nn.silu(gate) * up_part
    factor = hadamard.astype(jnp.float32)
    gathered = lax.all_to_all(
        hidden.astype(jnp.bfloat16), "hx", split_axis=0, concat_axis=1, tiled=True
    ).astype(hidden.dtype)
    row_count = gathered.shape[0]
    cube = gathered.reshape(row_count, HA, HB)
    cube = jnp.einsum("tab,ac->tcb", cube, sylvester(HA), precision=lax.Precision.HIGHEST)
    cube = jnp.einsum("tcb,bd->tcd", cube, factor, precision=lax.Precision.HIGHEST)
    turned = lax.all_to_all(
        cube.reshape(row_count, FF).astype(jnp.bfloat16),
        "hx",
        split_axis=1,
        concat_axis=0,
        tiled=True,
    ).astype(jnp.float32)
    rotated = (turned * (1.0 / math.sqrt(FF))).astype(jnp.bfloat16)
    summed = lax.psum_scatter(
        jnp.dot(rotated, down_codes, preferred_element_type=jnp.float32),
        "hx",
        scatter_dimension=0,
        tiled=True,
    )
    mixed = (summed * down_scales[None, :]).astype(jnp.bfloat16)
    return mixed


def solution(mesh):
    in_specs = (
        P(("groups", "hx"), None),
        P(None, "hx"),
        P(None, "hx"),
        P(None, "hx"),
        P(None, "hx"),
        P("hx", None),
        P(),
        P(),
    )
    out_specs = P(("groups", "hx"), None)
    return jax.shard_map(
        per_device, mesh=mesh, in_specs=in_specs, out_specs=out_specs, check_vma=False
    )
```

```python
import functools
import math

import jax
import jax.numpy as jnp
from jax import lax
from jax.experimental import pallas as pl
from jax.experimental.pallas import tpu as pltpu
from jax.sharding import PartitionSpec as P

HA = 512
HB = 52
FF = 26624


def sylvester(size):
    index_vec = jnp.arange(size, dtype=jnp.int32)
    parity = jnp.zeros((size, size), jnp.int32)
    for level in range(max(size.bit_length() - 1, 0)):
        left_bits = jnp.right_shift(index_vec[:, None], level) & 1
        right_bits = jnp.right_shift(index_vec[None, :], level) & 1
        parity = parity + left_bits * right_bits
    return (1 - 2 * (parity % 2)).astype(jnp.float32)


def dequantize(codes, scales):
    row_total, col_total = codes.shape
    group_total = scales.shape[0]
    grouped = codes.astype(jnp.float32).reshape(group_total, row_total // group_total, col_total)
    return (grouped * scales[:, None, :]).reshape(row_total, col_total).astype(jnp.bfloat16)


LANES = 128
WIDE = 2 * LANES
PIECES = 4
CHUNK = 512
SLOTS = 6
DOWN_COLS = 1024
DOWN_SLOTS = 3
BLOCK = 64
OUT_ROWS = 16


def kernel(
    n, groups, tok_ref, gate_ref, gscale_ref, up_ref, uscale_ref, down_ref, dscale_ref, had_ref,
    out_ref,
    ring, weights, dring, down, gs, us, ds, had, corner, table, local, tok_row, tok_f32, tok_out, tok, stage, lhs, acc,
    xsend, xrecv, zbuf, recv_z, rbuf, rot, part, pair_out, pair_in, sums, recv_c,
    ring_sem, load_sem, down_sem, tok_ssem, tok_rsem, fwd_ssem, fwd_rsem, x_ssem, x_rsem, z_ssem, z_rsem, r_ssem, r_rsem,
    p_ssem, p_rsem, c_ssem, c_rsem,
):
    f32, bf16, f8 = jnp.float32, jnp.bfloat16, jnp.float8_e4m3fn
    mine = lax.axis_index("groups")
    me = lax.axis_index("hx")
    chips = n // 2
    chip, core = lax.div(me, 2), lax.rem(me, 2)
    units = gate_ref.shape[1]
    tiles = units // LANES
    half_rows = gate_ref.shape[0] // groups
    chunks = half_rows // CHUNK
    piece_rows = tok.shape[3]
    down_chunks = down.shape[0]
    other = lax.rem(mine + 1, groups)

    def device(group, index):
        return {"groups": group, "hx": index}

    def remote(src, dst, send_sem, recv_sem, peer):
        return pltpu.make_async_remote_copy(
            src_ref=src, dst_ref=dst, send_sem=send_sem, recv_sem=recv_sem,
            device_id=peer, device_id_type=pl.DeviceIdType.MESH,
        )

    def chip_at(step):
        return lax.rem(chip + step, chips)

    partner = device(mine, chip * 2 + 1 - core)
    peers = [device(mine, lax.rem(me + step, n)) for step in range(1, n)]
    across = [device(other, chip_at(step) * 2 + core) for step in range(chips)]

    def start_weights(c, slot):
        rows = pl.ds(pl.multiple_of(mine * half_rows + c * CHUNK, CHUNK), CHUNK)
        for w, src in enumerate((gate_ref, up_ref)):
            pltpu.make_async_copy(src.at[rows], ring.at[slot, w], ring_sem.at[slot]).start()

    def wait_weights(slot):
        pltpu.make_async_copy(ring.at[slot], ring.at[slot], ring_sem.at[slot]).wait()

    def down_copy(c):
        cols = pl.ds(c * DOWN_COLS, DOWN_COLS)
        return pltpu.make_async_copy(down_ref.at[:, cols], dring.at[c % DOWN_SLOTS], down_sem.at[c % DOWN_SLOTS])

    scale_rows = gs.shape[0]
    half_scales = pl.ds(pl.multiple_of(mine * scale_rows, scale_rows), scale_rows)
    loads = [
        pltpu.make_async_copy(src, dst, load_sem.at[i])
        for i, (src, dst) in enumerate(
            (
                (tok_ref, tok_row), (had_ref, had), (dscale_ref, ds),
                (gscale_ref.at[half_scales], gs), (uscale_ref.at[half_scales], us),
            )
        )
    ]

    barrier = pltpu.get_barrier_semaphore()
    for peer in peers + across:
        pl.semaphore_signal(barrier, inc=1, device_id=peer, device_id_type=pl.DeviceIdType.MESH)
    for copy in loads:
        copy.start()

    def first(c, carry):
        start_weights(c, c)
        return carry

    lax.fori_loop(0, SLOTS, first, 0)
    loads[0].wait()
    row = tok_row[...].astype(f32)
    for k in range(tok_f32.shape[0]):
        tok_f32[k : k + 1, :] = row[:, k * LANES : (k + 1) * LANES]
    for h in range(groups):
        for p in range(PIECES):
            start = (h * PIECES + p) * piece_rows
            tok_out[h, p] = tok_f32[start : start + piece_rows, :].astype(bf16)
    for p in range(PIECES):
        tok[p, core, chip] = tok_out[mine, p]
    loads[1].wait()

    half = LANES // 2
    hb = had.shape[0]
    ha = units // hb
    corner[...] = jnp.zeros_like(corner)
    corner[:hb, :hb] = had[...].astype(f32)
    left_bits = lax.broadcasted_iota(jnp.int32, (ha, ha), 0) & lax.broadcasted_iota(jnp.int32, (ha, ha), 1)
    parity = jnp.zeros((ha, ha), jnp.int32)
    for level in range(ha.bit_length() - 1):
        parity = parity ^ (jnp.right_shift(left_bits, level) & 1)
    corner[half : half + ha, half : half + ha] = (1 - 2 * parity).astype(f32)

    def digits(unit):
        high = jnp.floor((unit + 0.5) * (1.0 / hb))
        return high, unit - hb * high

    at = lax.broadcasted_iota(jnp.int32, (LANES, LANES), 0).astype(f32)
    unit = lax.broadcasted_iota(jnp.int32, (LANES, LANES), 1).astype(f32)
    parts = corner[...].astype(bf16)
    for i in range(tiles):
        high, low = digits(unit + float(i * LANES))
        pick = jnp.where((at == low) | (at == high + half), 1.0, 0.0).astype(bf16)
        table[:, i * LANES : (i + 1) * LANES] = jnp.dot(parts, pick, preferred_element_type=f32).astype(bf16)
    factors = table[...]

    def build(i, carry):
        shape = (LANES, LANES)
        unit = (lax.broadcasted_iota(jnp.int32, shape, 0) + i * LANES).astype(f32)
        at = lax.broadcasted_iota(jnp.int32, shape, 1).astype(f32)
        high, low = digits(unit)
        pick = jnp.concatenate(
            [jnp.where(at == low, 1.0, 0.0), jnp.where(at == high + half, 1.0, 0.0)], axis=0
        ).astype(bf16)
        both = jnp.dot(pick, factors, preferred_element_type=f32)
        rows = pl.ds(pl.multiple_of(i * LANES, LANES), LANES)
        local[rows, :] = (both[:LANES] * both[LANES:]).astype(f8)
        return carry

    octet = 8 * hb
    lax.fori_loop(0, -(-octet // LANES), build, 0)

    def signs(k, carry):
        rows = pl.ds(pl.multiple_of(k * 32, 32), 32)
        base = local[rows, :].astype(bf16)
        for i in range(1, ha // 8):
            to = pl.ds(pl.multiple_of(i * octet + k * 32, 32), 32)
            local[to, :] = (base * table[half + 8 * i : half + 8 * i + 1, :]).astype(f8)
        return carry

    pl.semaphore_wait(barrier, len(peers) + len(across))

    hops = [(d, step) for d in range(groups) for step in range(chips) if (d, step) != (0, 0)]

    def tok_send(p, d, step):
        group = lax.rem(mine + d, groups)
        return remote(
            tok_out.at[group, p], tok.at[p, core, d * chips + chip], tok_ssem.at[p], tok_rsem.at[p],
            device(group, chip_at(step) * 2 + core),
        )

    def tok_all(p):
        blocks = pl.ds(0, len(hops))
        at = tok.at[p, core, blocks]
        return remote(at, at, tok_ssem.at[p], tok_rsem.at[p], partner)

    def forward(p, which):
        return remote(tok.at[p, which], tok.at[p, which], fwd_ssem.at[p], fwd_rsem.at[p], partner)

    for p in range(PIECES):
        for d, step in hops:
            tok_send(p, d, step).start()

    lhs[...] = jnp.zeros_like(lhs)
    acc[...] = jnp.zeros_like(acc)
    lax.fori_loop(0, octet // 32, signs, 0)

    def convert(c):
        wait_weights(c % SLOTS)

        def block(k, carry):
            rows = pl.ds(pl.multiple_of(k * BLOCK, BLOCK), BLOCK)
            to = pl.ds(pl.multiple_of(c * CHUNK + k * BLOCK, BLOCK), BLOCK)
            for w in range(2):
                weights[w, to, :] = ring[c % SLOTS, w, rows, :].astype(f8)
            return carry

        lax.fori_loop(0, CHUNK // BLOCK, block, 0)
        if c + SLOTS < chunks:
            start_weights(c + SLOTS, c % SLOTS)
        elif c + SLOTS - chunks < DOWN_SLOTS:
            down_copy(c + SLOTS - chunks).start()

    def convert_down(c):
        down_copy(c).wait()

        def block(k, carry):
            rows = pl.ds(pl.multiple_of(k * BLOCK, BLOCK), BLOCK)
            down[c, rows, :] = dring[c % DOWN_SLOTS, rows, :].astype(f8)
            return carry

        lax.fori_loop(0, units // BLOCK, block, 0)
        if c + DOWN_SLOTS < down_chunks:
            down_copy(c + DOWN_SLOTS).start()

    def relay(p):
        tok_all(p).wait_recv()
        forward(p, core).start()

    def ready(p):
        forward(p, 1 - core).wait_recv()
        stage[...] = tok[p].reshape(stage.shape).astype(f32)
        for k in range(piece_rows):
            part_rows = [
                stage[pl.ds(w * n * piece_rows + k, n, stride=piece_rows), :] for w in range(2)
            ]
            both = jnp.concatenate(
                [part_rows[0][:chips], part_rows[1][:chips], part_rows[0][chips:], part_rows[1][chips:]], axis=0
            ).astype(bf16)
            q, odd = divmod(k, 2)
            lhs[q, odd * 2 * n : (odd + 1) * 2 * n, odd * LANES : (odd + 1) * LANES] = both

    def products(p, cols, tail):
        sums_now = [None, None]
        for q in range(piece_rows // 2):
            left = lhs[q]
            row = p * piece_rows + 2 * q
            rows = slice(row * LANES, (row + 2) * LANES)
            if tail:
                right = jnp.concatenate([weights[0, rows, cols], weights[1, rows, cols]], axis=1)
                scale = jnp.concatenate([gs[row : row + 2, cols], us[row : row + 2, cols]], axis=1)
                sides = [(right, scale)]
            else:
                sides = [(weights[w, rows, cols], scale[row : row + 2, cols]) for w, scale in ((0, gs), (1, us))]
            for w, (right, scale) in enumerate(sides):
                res = jnp.dot(left, right, preferred_element_type=f32)
                new = res[: 2 * n] * scale[0:1, :] + res[2 * n :] * scale[1:2, :]
                sums_now[w] = new if sums_now[w] is None else sums_now[w] + new
        if tail:
            width = sums_now[0].shape[1] // 2
            return sums_now[0][:, :width], sums_now[0][:, width:]
        return sums_now

    spans = [(at, min(WIDE, units - at)) for at in range(0, units, WIDE)]

    def x_send(j, width):
        at = (j, slice(None), slice(None), pl.ds(0, width))
        return remote(xsend.at[at], xrecv.at[at], x_ssem.at[j], x_rsem.at[j], across[0])

    def run(p):
        for j, (at, width) in enumerate(spans):
            cols = slice(at, at + width)
            pair = products(p, cols, width < WIDE)
            for w in range(2):
                if p + 1 < PIECES:
                    acc[w, :, cols] += pair[w]
                else:
                    total = acc[w, :, cols] + pair[w]
                    acc[w, :n, cols] = total[:n]
                    xsend[j, w, :, :width] = total[n:].astype(bf16)
            if p + 1 == PIECES:
                x_send(j, width).start()

    for copy in loads[2:]:
        copy.wait()
    early = chunks - 2
    for c in range(early):
        convert(c)
    relay(0)
    convert(early)
    relay(1)
    convert(early + 1)
    for p in range(PIECES):
        ready(p)
        run(p)
        if p + 2 < PIECES:
            relay(p + 2)

    for c in range(3):
        convert_down(c)
    turned = None
    for j, (at, width) in enumerate(spans):
        x_send(j, width).wait_recv()
        cols = slice(at, at + width)
        gate = acc[0, :n, cols] + xrecv[j, 0, :, :width].astype(f32)
        lift = acc[1, :n, cols] + xrecv[j, 1, :, :width].astype(f32)
        hidden = (gate / (1.0 + jnp.exp(-gate)) * lift).astype(bf16)
        new = jnp.dot(hidden, local[cols, :], preferred_element_type=f32)
        turned = new if turned is None else turned + new
    turned = turned.astype(bf16)

    owners = zbuf.shape[0]
    quarter = n // 4

    def owner_at(o):
        return quarter + (o % 2) * quarter + o // 2

    def held(o):
        return len(range(o, tiles, owners))

    for j in range(tiles):
        zbuf[j % owners, j // owners] = turned[:, j * LANES : (j + 1) * LANES]

    def z_out(o):
        count = pl.ds(0, held(o))
        return remote(
            zbuf.at[o, count], recv_z.at[me, count], z_ssem.at[o], z_rsem.at[0], device(mine, owner_at(o))
        )

    for o in range(owners):

        @pl.when(me != owner_at(o))
        def _():
            z_out(o).start()

        @pl.when(me == owner_at(o))
        def _():
            recv_z[me] = zbuf[o]

    for c in range(3, 6):
        convert_down(c)

    place = me - quarter
    number = lax.rem(place, quarter) * 2 + lax.div(place, quarter)
    owns = jnp.logical_and(me >= quarter, me < 3 * quarter)
    extra = tiles % owners
    scale = 1.0 / math.sqrt(units * n)

    def r_out(i, count):
        at = pl.ds(0, count)
        peer = lax.rem(me + i, n)
        return remote(rbuf.at[peer, at], rot.at[number, at], r_ssem.at[0], r_rsem.at[number], device(mine, peer))

    def turn(count):
        at = pl.ds(0, count)
        every = recv_z.at[pl.ds(0, n - 1), at]
        remote(every, every, z_ssem.at[0], z_rsem.at[0], partner).wait_recv()
        for t in range(count):
            cube = [recv_z[h, t].astype(f32) for h in range(n)]
            span = 1
            while span < n:
                nxt = list(cube)
                for h in range(n):
                    if h & span == 0:
                        nxt[h] = cube[h] + cube[h | span]
                        nxt[h | span] = cube[h] - cube[h | span]
                cube = nxt
                span *= 2
            for h in range(n):
                rbuf[h, t] = (cube[h] * scale).astype(bf16)
        for i in range(1, n):
            r_out(i, count).start()
        rot[number] = rbuf[me]

    many, few = held(0), held(owners - 1)

    def by_count(action):
        if extra == 0:
            pl.when(owns)(lambda: action(many))
        else:
            pl.when(jnp.logical_and(owns, number < extra))(lambda: action(many))
            pl.when(jnp.logical_and(owns, number >= extra))(lambda: action(few))

    by_count(turn)

    for c in range(6, down_chunks):
        convert_down(c)

    for o in range(owners):

        @pl.when(me != owner_at(o))
        def _():
            count = pl.ds(0, held(o))
            remote(
                rbuf.at[0, count], rot.at[o, count], r_ssem.at[0], r_rsem.at[o], device(mine, owner_at(o))
            ).wait_recv()

    rotated = jnp.concatenate([rot[j % owners, j // owners] for j in range(tiles)], axis=1)

    out_pieces = recv_c.shape[0]
    per_piece = down_chunks // out_pieces
    blocks = DOWN_COLS // LANES
    own_rows = chips * OUT_ROWS

    def pair_copy(p, which):
        at = pl.ds(which * chips, chips)
        return remote(pair_out.at[p, at], pair_in.at[p], p_ssem.at[p], p_rsem.at[p], partner)

    def c_out(p, step):
        to = chip_at(step)
        return remote(
            sums.at[p, to], recv_c.at[p, chip], c_ssem.at[p], c_rsem.at[p], device(mine, to * 2 + core)
        )

    def c_all(p, ref):
        at = ref.at[p, pl.ds(0, chips - 1)]
        return remote(at, at, c_ssem.at[p], c_rsem.at[p], partner)

    def finish(p):
        pair_copy(p, core).wait_recv()
        rows = pl.ds(pl.multiple_of(core * own_rows, own_rows), own_rows)
        both = part[p, rows, :] + pair_in[p].reshape(own_rows, LANES).astype(f32)
        sums[p] = both.astype(bf16).reshape(chips, OUT_ROWS, LANES)
        for step in range(1, chips):
            c_out(p, step).start()
        recv_c[p, chip] = sums[p, chip]

    for p in range(out_pieces):
        for k in range(per_piece):
            res = jnp.dot(rotated, down[p * per_piece + k], preferred_element_type=f32)
            for b in range(blocks):
                part[p, pl.ds(k * blocks + b, n, stride=OUT_ROWS), :] = res[:, b * LANES : (b + 1) * LANES]
        pair_out[p] = part[p].astype(bf16).reshape(n, OUT_ROWS, LANES)
        pair_copy(p, 1 - core).start()
        if p > 0:
            finish(p - 1)
    finish(out_pieces - 1)

    for p in range(out_pieces):
        c_all(p, recv_c).wait_recv()
        total = recv_c[p, 0].astype(f32)
        for h in range(1, chips):
            total = total + recv_c[p, h].astype(f32)
        for r in range(OUT_ROWS):
            cols = slice((p * OUT_ROWS + r) * LANES, (p * OUT_ROWS + r + 1) * LANES)
            out_ref[:, cols] = (total[r : r + 1, :] * ds[:, cols]).astype(out_ref.dtype)

    for p in range(PIECES):
        tok_all(p).wait_send()
        forward(p, core).wait_send()
    for j, (at, width) in enumerate(spans):
        x_send(j, width).wait_send()
    for o in range(owners):

        @pl.when(me != owner_at(o))
        def _():
            z_out(o).wait_send()

    def drain(count):
        every = rbuf.at[pl.ds(0, n - 1), pl.ds(0, count)]
        remote(every, every, r_ssem.at[0], r_rsem.at[0], partner).wait_send()

    by_count(drain)
    for p in range(out_pieces):
        pair_copy(p, 1 - core).wait_send()
        c_all(p, sums).wait_send()


def fused(n, groups, tokens, gate_codes, gate_scales, up_codes, up_scales, down_codes, down_scales, hadamard):
    depth, units = gate_codes.shape
    width = down_codes.shape[1]
    tiles = units // LANES
    piece_rows = depth // (groups * PIECES * LANES)
    half_scales = (gate_scales.shape[0] // groups, units)
    out_pieces = width // (LANES * OUT_ROWS)
    owners = n // 2
    held = -(-tiles // owners)
    spans = -(-units // WIDE)
    chips = n // 2
    bf16, f32, f8 = jnp.bfloat16, jnp.float32, jnp.float8_e4m3fn
    dma = pltpu.SemaphoreType.DMA
    vmem = pltpu.VMEM
    return pl.pallas_call(
        functools.partial(kernel, n, groups),
        out_shape=jax.ShapeDtypeStruct((1, width), bf16),
        in_specs=[pl.BlockSpec(memory_space=pl.ANY)] * 8,
        out_specs=pl.BlockSpec(memory_space=pltpu.VMEM),
        scratch_shapes=[
            vmem((SLOTS, 2, CHUNK, units), bf16),
            vmem((2, depth // groups, units), f8),
            vmem((DOWN_SLOTS, units, DOWN_COLS), bf16),
            vmem((width // DOWN_COLS, units, DOWN_COLS), f8),
            vmem(half_scales, f32),
            vmem(half_scales, f32),
            vmem((1, width), f32),
            vmem(hadamard.shape, hadamard.dtype),
            vmem((LANES, LANES), f32),
            vmem((LANES, units), bf16),
            vmem((units, units), f8),
            vmem((1, depth), bf16),
            vmem((depth // LANES, LANES), f32),
            vmem((groups, PIECES, piece_rows, LANES), bf16),
            vmem((PIECES, 2, n, piece_rows, LANES), bf16),
            vmem((2 * n * piece_rows, LANES), f32),
            vmem((piece_rows // 2, 4 * n, WIDE), bf16),
            vmem((2, 2 * n, units), f32),
            vmem((spans, 2, n, WIDE), bf16),
            vmem((spans, 2, n, WIDE), bf16),
            vmem((owners, held, n, LANES), bf16),
            vmem((n, held, n, LANES), bf16),
            vmem((n, held, n, LANES), bf16),
            vmem((owners, held, n, LANES), bf16),
            vmem((out_pieces, n * OUT_ROWS, LANES), f32),
            vmem((out_pieces, n, OUT_ROWS, LANES), bf16),
            vmem((out_pieces, chips, OUT_ROWS, LANES), bf16),
            vmem((out_pieces, chips, OUT_ROWS, LANES), bf16),
            vmem((out_pieces, chips, OUT_ROWS, LANES), bf16),
            dma((SLOTS,)),
            dma((5,)),
            dma((DOWN_SLOTS,)),
            dma((PIECES,)),
            dma((PIECES,)),
            dma((PIECES,)),
            dma((PIECES,)),
            dma((spans,)),
            dma((spans,)),
            dma((owners,)),
            dma((1,)),
            dma((1,)),
            dma((owners,)),
            dma((out_pieces,)),
            dma((out_pieces,)),
            dma((out_pieces,)),
            dma((out_pieces,)),
        ],
        compiler_params=pltpu.CompilerParams(
            collective_id=0, has_side_effects=True, vmem_limit_bytes=67043328
        ),
    )(
        tokens, gate_codes, gate_scales, up_codes, up_scales, down_codes, down_scales.reshape(1, width), hadamard,
    )


def fits(n, groups, tokens, gate_scales, down_codes):
    rows, depth = tokens.shape
    units, width = down_codes.shape
    scale_rows = gate_scales.shape[0]
    return (
        rows == 1
        and n == 16
        and groups == 2
        and HA % n == 0
        and units * n == HA * HB
        and HA // n <= LANES // 2
        and HB <= LANES // 2
        and HA // n % 8 == 0
        and 8 * HB % 32 == 0
        and depth == scale_rows * LANES
        and scale_rows % (groups * PIECES * 8) == 0
        and depth == 8 * groups * CHUNK
        and width == 8 * DOWN_COLS
        and units % LANES == 0
        and n // 2 <= units // LANES <= n
    )


def per_device(
    tokens, gate_codes, gate_scales, up_codes, up_scales, down_codes, down_scales, hadamard
):
    n = lax.axis_size("hx")
    groups = lax.axis_size("groups")
    if fits(n, groups, tokens, gate_scales, down_codes):
        return fused(
            n, groups, tokens, gate_codes, gate_scales, up_codes, up_scales, down_codes, down_scales, hadamard
        )
    gate_weight = dequantize(gate_codes, gate_scales)
    up_weight = dequantize(up_codes, up_scales)
    tile_rows = lax.all_gather(tokens, "hx", axis=0, tiled=True)
    gate = jnp.dot(tile_rows, gate_weight, preferred_element_type=jnp.float32)
    up_part = jnp.dot(tile_rows, up_weight, preferred_element_type=jnp.float32)
    hidden = jax.nn.silu(gate) * up_part
    factor = hadamard.astype(jnp.float32)
    gathered = lax.all_to_all(
        hidden.astype(jnp.bfloat16), "hx", split_axis=0, concat_axis=1, tiled=True
    ).astype(hidden.dtype)
    row_count = gathered.shape[0]
    cube = gathered.reshape(row_count, HA, HB)
    cube = jnp.einsum("tab,ac->tcb", cube, sylvester(HA), precision=lax.Precision.HIGHEST)
    cube = jnp.einsum("tcb,bd->tcd", cube, factor, precision=lax.Precision.HIGHEST)
    turned = lax.all_to_all(
        cube.reshape(row_count, FF).astype(jnp.bfloat16),
        "hx",
        split_axis=1,
        concat_axis=0,
        tiled=True,
    ).astype(jnp.float32)
    rotated = (turned * (1.0 / math.sqrt(FF))).astype(jnp.bfloat16)
    summed = lax.psum_scatter(
        jnp.dot(rotated, down_codes, preferred_element_type=jnp.float32),
        "hx",
        scatter_dimension=0,
        tiled=True,
    )
    mixed = (summed * down_scales[None, :]).astype(jnp.bfloat16)
    return mixed


def solution(mesh):
    in_specs = (
        P(("groups", "hx"), None),
        P(None, "hx"),
        P(None, "hx"),
        P(None, "hx"),
        P(None, "hx"),
        P("hx", None),
        P(),
        P(),
    )
    out_specs = P(("groups", "hx"), None)
    return jax.shard_map(
        per_device, mesh=mesh, in_specs=in_specs, out_specs=out_specs, check_vma=False
    )
```

```python
import functools
import math

import jax
import jax.numpy as jnp
from jax import lax
from jax.experimental import pallas as pl
from jax.experimental.pallas import tpu as pltpu
from jax.sharding import PartitionSpec as P

HA = 512
HB = 52
FF = 26624


def sylvester(size):
    index_vec = jnp.arange(size, dtype=jnp.int32)
    parity = jnp.zeros((size, size), jnp.int32)
    for level in range(max(size.bit_length() - 1, 0)):
        left_bits = jnp.right_shift(index_vec[:, None], level) & 1
        right_bits = jnp.right_shift(index_vec[None, :], level) & 1
        parity = parity + left_bits * right_bits
    return (1 - 2 * (parity % 2)).astype(jnp.float32)


def dequantize(codes, scales):
    row_total, col_total = codes.shape
    group_total = scales.shape[0]
    grouped = codes.astype(jnp.float32).reshape(group_total, row_total // group_total, col_total)
    return (grouped * scales[:, None, :]).reshape(row_total, col_total).astype(jnp.bfloat16)


LANES = 128
WIDE = 2 * LANES
PIECES = 2
MERGED = 1
CHUNK = 512
SLOTS = 6
DOWN_COLS = 1024
DOWN_SLOTS = 3
BLOCK = 64
OUT_ROWS = 16


def kernel(
    n, groups, tok_ref, gate_ref, gscale_ref, up_ref, uscale_ref, down_ref, dscale_ref, had_ref,
    out_ref,
    ring, weights, dring, down, gs, us, ds, had, corner, table, local, tok_row, tok_f32, tok_out, tok, stage, lhs, acc,
    xsend, xrecv, zbuf, recv_z, rbuf, rot, part, pair_out, pair_in, sums, recv_c,
    ring_sem, load_sem, down_sem, tok_ssem, tok_rsem, fwd_ssem, fwd_rsem, x_ssem, x_rsem, z_ssem, z_rsem, r_ssem, r_rsem,
    p_ssem, p_rsem, c_ssem, c_rsem,
):
    f32, bf16, f8 = jnp.float32, jnp.bfloat16, jnp.float8_e4m3fn
    mine = lax.axis_index("groups")
    me = lax.axis_index("hx")
    chips = n // 2
    chip, core = lax.div(me, 2), lax.rem(me, 2)
    units = gate_ref.shape[1]
    tiles = units // LANES
    half_rows = gate_ref.shape[0] // groups
    chunks = half_rows // CHUNK
    piece_rows = tok.shape[3]
    down_chunks = down.shape[0]
    other = lax.rem(mine + 1, groups)

    def device(group, index):
        return {"groups": group, "hx": index}

    def remote(src, dst, send_sem, recv_sem, peer):
        return pltpu.make_async_remote_copy(
            src_ref=src, dst_ref=dst, send_sem=send_sem, recv_sem=recv_sem,
            device_id=peer, device_id_type=pl.DeviceIdType.MESH,
        )

    def chip_at(step):
        return lax.rem(chip + step, chips)

    partner = device(mine, chip * 2 + 1 - core)
    peers = [device(mine, lax.rem(me + step, n)) for step in range(1, n)]
    across = [device(other, chip_at(step) * 2 + core) for step in range(chips)]

    def start_weights(c, slot):
        rows = pl.ds(pl.multiple_of(mine * half_rows + c * CHUNK, CHUNK), CHUNK)
        for w, src in enumerate((gate_ref, up_ref)):
            pltpu.make_async_copy(src.at[rows], ring.at[slot, w], ring_sem.at[slot]).start()

    def wait_weights(slot):
        pltpu.make_async_copy(ring.at[slot], ring.at[slot], ring_sem.at[slot]).wait()

    def down_copy(c):
        cols = pl.ds(c * DOWN_COLS, DOWN_COLS)
        return pltpu.make_async_copy(down_ref.at[:, cols], dring.at[c % DOWN_SLOTS], down_sem.at[c % DOWN_SLOTS])

    scale_rows = gs.shape[0]
    half_scales = pl.ds(pl.multiple_of(mine * scale_rows, scale_rows), scale_rows)
    loads = [
        pltpu.make_async_copy(src, dst, load_sem.at[i])
        for i, (src, dst) in enumerate(
            (
                (tok_ref, tok_row), (had_ref, had), (dscale_ref, ds),
                (gscale_ref.at[half_scales], gs), (uscale_ref.at[half_scales], us),
            )
        )
    ]

    barrier = pltpu.get_barrier_semaphore()
    for peer in peers + across:
        pl.semaphore_signal(barrier, inc=1, device_id=peer, device_id_type=pl.DeviceIdType.MESH)
    for copy in loads:
        copy.start()

    def first(c, carry):
        start_weights(c, c)
        return carry

    lax.fori_loop(0, SLOTS, first, 0)
    loads[0].wait()
    row = tok_row[...].astype(f32)
    for k in range(tok_f32.shape[0]):
        tok_f32[k : k + 1, :] = row[:, k * LANES : (k + 1) * LANES]
    for h in range(groups):
        for p in range(PIECES):
            start = (h * PIECES + p) * piece_rows
            tok_out[h, p] = tok_f32[start : start + piece_rows, :].astype(bf16)
    for p in range(PIECES):
        tok[p, core, chip] = tok_out[mine, p]
    loads[1].wait()

    half = LANES // 2
    hb = had.shape[0]
    ha = units // hb
    corner[...] = jnp.zeros_like(corner)
    corner[:hb, :hb] = had[...].astype(f32)
    left_bits = lax.broadcasted_iota(jnp.int32, (ha, ha), 0) & lax.broadcasted_iota(jnp.int32, (ha, ha), 1)
    parity = jnp.zeros((ha, ha), jnp.int32)
    for level in range(ha.bit_length() - 1):
        parity = parity ^ (jnp.right_shift(left_bits, level) & 1)
    corner[half : half + ha, half : half + ha] = (1 - 2 * parity).astype(f32)

    def digits(unit):
        high = jnp.floor((unit + 0.5) * (1.0 / hb))
        return high, unit - hb * high

    at = lax.broadcasted_iota(jnp.int32, (LANES, LANES), 0).astype(f32)
    unit = lax.broadcasted_iota(jnp.int32, (LANES, LANES), 1).astype(f32)
    parts = corner[...].astype(bf16)
    for i in range(tiles):
        high, low = digits(unit + float(i * LANES))
        pick = jnp.where((at == low) | (at == high + half), 1.0, 0.0).astype(bf16)
        table[:, i * LANES : (i + 1) * LANES] = jnp.dot(parts, pick, preferred_element_type=f32).astype(bf16)
    factors = table[...]

    def build(i, carry):
        shape = (LANES, LANES)
        unit = (lax.broadcasted_iota(jnp.int32, shape, 0) + i * LANES).astype(f32)
        at = lax.broadcasted_iota(jnp.int32, shape, 1).astype(f32)
        high, low = digits(unit)
        pick = jnp.concatenate(
            [jnp.where(at == low, 1.0, 0.0), jnp.where(at == high + half, 1.0, 0.0)], axis=0
        ).astype(bf16)
        both = jnp.dot(pick, factors, preferred_element_type=f32)
        rows = pl.ds(pl.multiple_of(i * LANES, LANES), LANES)
        local[rows, :] = (both[:LANES] * both[LANES:]).astype(f8)
        return carry

    octet = 8 * hb
    lax.fori_loop(0, -(-octet // LANES), build, 0)

    def signs(k, carry):
        rows = pl.ds(pl.multiple_of(k * 32, 32), 32)
        base = local[rows, :].astype(bf16)
        for i in range(1, ha // 8):
            to = pl.ds(pl.multiple_of(i * octet + k * 32, 32), 32)
            local[to, :] = (base * table[half + 8 * i : half + 8 * i + 1, :]).astype(f8)
        return carry

    pl.semaphore_wait(barrier, len(peers) + len(across))

    hops = [(d, step) for d in range(groups) for step in range(chips) if (d, step) != (0, 0)]

    def tok_send(p, d, step):
        group = lax.rem(mine + d, groups)
        return remote(
            tok_out.at[group, p], tok.at[p, core, d * chips + chip], tok_ssem.at[p], tok_rsem.at[p],
            device(group, chip_at(step) * 2 + core),
        )

    def tok_all(p):
        blocks = pl.ds(0, len(hops))
        at = tok.at[p, core, blocks]
        return remote(at, at, tok_ssem.at[p], tok_rsem.at[p], partner)

    def forward(p, which):
        return remote(tok.at[p, which], tok.at[p, which], fwd_ssem.at[p], fwd_rsem.at[p], partner)

    for p in range(PIECES):
        for d, step in hops:
            tok_send(p, d, step).start()

    lhs[...] = jnp.zeros_like(lhs)
    acc[...] = jnp.zeros_like(acc)
    lax.fori_loop(0, octet // 32, signs, 0)

    def convert(c):
        wait_weights(c % SLOTS)

        def block(k, carry):
            rows = pl.ds(pl.multiple_of(k * BLOCK, BLOCK), BLOCK)
            to = pl.ds(pl.multiple_of(c * CHUNK + k * BLOCK, BLOCK), BLOCK)
            for w in range(2):
                weights[w, to, :] = ring[c % SLOTS, w, rows, :].astype(f8)
            return carry

        lax.fori_loop(0, CHUNK // BLOCK, block, 0)
        if c + SLOTS < chunks:
            start_weights(c + SLOTS, c % SLOTS)
        elif c + SLOTS - chunks < DOWN_SLOTS:
            down_copy(c + SLOTS - chunks).start()

    def convert_down(c):
        down_copy(c).wait()

        def block(k, carry):
            rows = pl.ds(pl.multiple_of(k * BLOCK, BLOCK), BLOCK)
            down[c, rows, :] = dring[c % DOWN_SLOTS, rows, :].astype(f8)
            return carry

        lax.fori_loop(0, units // BLOCK, block, 0)
        if c + DOWN_SLOTS < down_chunks:
            down_copy(c + DOWN_SLOTS).start()

    def relay(p):
        tok_all(p).wait_recv()
        forward(p, core).start()

    def ready(p):
        forward(p, 1 - core).wait_recv()
        stage[...] = tok[p].reshape(stage.shape).astype(f32)
        for k in range(piece_rows):
            part_rows = [
                stage[pl.ds(w * n * piece_rows + k, n, stride=piece_rows), :] for w in range(2)
            ]
            both = jnp.concatenate(
                [part_rows[0][:chips], part_rows[1][:chips], part_rows[0][chips:], part_rows[1][chips:]], axis=0
            ).astype(bf16)
            q, odd = divmod(k, 2)
            lhs[p, q, odd * 2 * n : (odd + 1) * 2 * n, odd * LANES : (odd + 1) * LANES] = both

    def products(p, cols, tail):
        sums_now = [None, None]
        for q in range(piece_rows // 2):
            left = lhs[p, q]
            row = p * piece_rows + 2 * q
            rows = slice(row * LANES, (row + 2) * LANES)
            if tail:
                right = jnp.concatenate([weights[0, rows, cols], weights[1, rows, cols]], axis=1)
                scale = jnp.concatenate([gs[row : row + 2, cols], us[row : row + 2, cols]], axis=1)
                sides = [(right, scale)]
            else:
                sides = [(weights[w, rows, cols], scale[row : row + 2, cols]) for w, scale in ((0, gs), (1, us))]
            for w, (right, scale) in enumerate(sides):
                res = jnp.dot(left, right, preferred_element_type=f32)
                new = res[: 2 * n] * scale[0:1, :] + res[2 * n :] * scale[1:2, :]
                sums_now[w] = new if sums_now[w] is None else sums_now[w] + new
        if tail:
            width = sums_now[0].shape[1] // 2
            return sums_now[0][:, :width], sums_now[0][:, width:]
        return sums_now

    spans = [(at, min(WIDE, units - at)) for at in range(0, units, WIDE)]

    def x_send(j, width):
        at = (j, slice(None), slice(None), pl.ds(0, width))
        return remote(xsend.at[at], xrecv.at[at], x_ssem.at[j], x_rsem.at[j], across[0])

    def run(pieces):
        final = pieces[-1] + 1 == PIECES
        for j, (at, width) in enumerate(spans):
            cols = slice(at, at + width)
            pair = None
            for p in pieces:
                new = products(p, cols, width < WIDE)
                pair = new if pair is None else [a + b for a, b in zip(pair, new)]
            for w in range(2):
                if not final:
                    acc[w, :, cols] += pair[w]
                else:
                    total = acc[w, :, cols] + pair[w]
                    acc[w, :n, cols] = total[:n]
                    xsend[j, w, :, :width] = total[n:].astype(bf16)
            if final:
                x_send(j, width).start()

    for copy in loads[2:]:
        copy.wait()
    per_piece = chunks // PIECES
    last = PIECES - MERGED
    early = chunks - per_piece
    for c in range(early):
        convert(c)
    relay(0)
    convert(early)
    relay(1)
    for p in range(PIECES):
        ready(p)
        if p < last:
            run([p])
        if p + 2 < PIECES:
            relay(p + 2)
        if p == 0:
            for c in range(early + 1, chunks):
                convert(c)
    run(list(range(last, PIECES)))

    for c in range(3):
        convert_down(c)
    turned = None
    for j, (at, width) in enumerate(spans):
        x_send(j, width).wait_recv()
        cols = slice(at, at + width)
        gate = acc[0, :n, cols] + xrecv[j, 0, :, :width].astype(f32)
        lift = acc[1, :n, cols] + xrecv[j, 1, :, :width].astype(f32)
        hidden = (gate / (1.0 + jnp.exp(-gate)) * lift).astype(bf16)
        new = jnp.dot(hidden, local[cols, :], preferred_element_type=f32)
        turned = new if turned is None else turned + new
    turned = turned.astype(bf16)

    owners = zbuf.shape[0]
    quarter = n // 4

    def owner_at(o):
        return quarter + (o % 2) * quarter + o // 2

    def held(o):
        return len(range(o, tiles, owners))

    for j in range(tiles):
        zbuf[j % owners, j // owners] = turned[:, j * LANES : (j + 1) * LANES]

    def z_out(o):
        count = pl.ds(0, held(o))
        return remote(
            zbuf.at[o, count], recv_z.at[me, count], z_ssem.at[o], z_rsem.at[0], device(mine, owner_at(o))
        )

    for o in range(owners):

        @pl.when(me != owner_at(o))
        def _():
            z_out(o).start()

        @pl.when(me == owner_at(o))
        def _():
            recv_z[me] = zbuf[o]

    for c in range(3, 6):
        convert_down(c)

    place = me - quarter
    number = lax.rem(place, quarter) * 2 + lax.div(place, quarter)
    owns = jnp.logical_and(me >= quarter, me < 3 * quarter)
    extra = tiles % owners
    scale = 1.0 / math.sqrt(units * n)

    def r_out(i, count):
        at = pl.ds(0, count)
        peer = lax.rem(me + i, n)
        return remote(rbuf.at[peer, at], rot.at[number, at], r_ssem.at[0], r_rsem.at[number], device(mine, peer))

    def turn(count):
        at = pl.ds(0, count)
        every = recv_z.at[pl.ds(0, n - 1), at]
        remote(every, every, z_ssem.at[0], z_rsem.at[0], partner).wait_recv()
        for t in range(count):
            cube = [recv_z[h, t].astype(f32) for h in range(n)]
            span = 1
            while span < n:
                nxt = list(cube)
                for h in range(n):
                    if h & span == 0:
                        nxt[h] = cube[h] + cube[h | span]
                        nxt[h | span] = cube[h] - cube[h | span]
                cube = nxt
                span *= 2
            for h in range(n):
                rbuf[h, t] = (cube[h] * scale).astype(bf16)
        for i in range(1, n):
            r_out(i, count).start()
        rot[number] = rbuf[me]

    many, few = held(0), held(owners - 1)

    def by_count(action):
        if extra == 0:
            pl.when(owns)(lambda: action(many))
        else:
            pl.when(jnp.logical_and(owns, number < extra))(lambda: action(many))
            pl.when(jnp.logical_and(owns, number >= extra))(lambda: action(few))

    by_count(turn)

    for c in range(6, down_chunks):
        convert_down(c)

    for o in range(owners):

        @pl.when(me != owner_at(o))
        def _():
            count = pl.ds(0, held(o))
            remote(
                rbuf.at[0, count], rot.at[o, count], r_ssem.at[0], r_rsem.at[o], device(mine, owner_at(o))
            ).wait_recv()

    rotated = jnp.concatenate([rot[j % owners, j // owners] for j in range(tiles)], axis=1)

    out_pieces = recv_c.shape[0]
    per_out = down_chunks // out_pieces
    blocks = DOWN_COLS // LANES
    own_rows = chips * OUT_ROWS

    def pair_copy(p, which):
        at = pl.ds(which * chips, chips)
        return remote(pair_out.at[p, at], pair_in.at[p], p_ssem.at[p], p_rsem.at[p], partner)

    def c_out(p, step):
        to = chip_at(step)
        return remote(
            sums.at[p, to], recv_c.at[p, chip], c_ssem.at[p], c_rsem.at[p], device(mine, to * 2 + core)
        )

    def c_all(p, ref):
        at = ref.at[p, pl.ds(0, chips - 1)]
        return remote(at, at, c_ssem.at[p], c_rsem.at[p], partner)

    def finish(p):
        pair_copy(p, core).wait_recv()
        rows = pl.ds(pl.multiple_of(core * own_rows, own_rows), own_rows)
        both = part[p, rows, :] + pair_in[p].reshape(own_rows, LANES).astype(f32)
        sums[p] = both.astype(bf16).reshape(chips, OUT_ROWS, LANES)
        for step in range(1, chips):
            c_out(p, step).start()
        recv_c[p, chip] = sums[p, chip]

    for p in range(out_pieces):
        for k in range(per_out):
            res = jnp.dot(rotated, down[p * per_out + k], preferred_element_type=f32)
            for b in range(blocks):
                part[p, pl.ds(k * blocks + b, n, stride=OUT_ROWS), :] = res[:, b * LANES : (b + 1) * LANES]
        pair_out[p] = part[p].astype(bf16).reshape(n, OUT_ROWS, LANES)
        pair_copy(p, 1 - core).start()
        if p > 0:
            finish(p - 1)
    finish(out_pieces - 1)

    for p in range(out_pieces):
        c_all(p, recv_c).wait_recv()
        total = recv_c[p, 0].astype(f32)
        for h in range(1, chips):
            total = total + recv_c[p, h].astype(f32)
        for r in range(OUT_ROWS):
            cols = slice((p * OUT_ROWS + r) * LANES, (p * OUT_ROWS + r + 1) * LANES)
            out_ref[:, cols] = (total[r : r + 1, :] * ds[:, cols]).astype(out_ref.dtype)

    for p in range(PIECES):
        tok_all(p).wait_send()
        forward(p, core).wait_send()
    for j, (at, width) in enumerate(spans):
        x_send(j, width).wait_send()
    for o in range(owners):

        @pl.when(me != owner_at(o))
        def _():
            z_out(o).wait_send()

    def drain(count):
        every = rbuf.at[pl.ds(0, n - 1), pl.ds(0, count)]
        remote(every, every, r_ssem.at[0], r_rsem.at[0], partner).wait_send()

    by_count(drain)
    for p in range(out_pieces):
        pair_copy(p, 1 - core).wait_send()
        c_all(p, sums).wait_send()


def fused(n, groups, tokens, gate_codes, gate_scales, up_codes, up_scales, down_codes, down_scales, hadamard):
    depth, units = gate_codes.shape
    width = down_codes.shape[1]
    tiles = units // LANES
    piece_rows = depth // (groups * PIECES * LANES)
    half_scales = (gate_scales.shape[0] // groups, units)
    out_pieces = width // (LANES * OUT_ROWS)
    owners = n // 2
    held = -(-tiles // owners)
    spans = -(-units // WIDE)
    chips = n // 2
    bf16, f32, f8 = jnp.bfloat16, jnp.float32, jnp.float8_e4m3fn
    dma = pltpu.SemaphoreType.DMA
    vmem = pltpu.VMEM
    return pl.pallas_call(
        functools.partial(kernel, n, groups),
        out_shape=jax.ShapeDtypeStruct((1, width), bf16),
        in_specs=[pl.BlockSpec(memory_space=pl.ANY)] * 8,
        out_specs=pl.BlockSpec(memory_space=pltpu.VMEM),
        scratch_shapes=[
            vmem((SLOTS, 2, CHUNK, units), bf16),
            vmem((2, depth // groups, units), f8),
            vmem((DOWN_SLOTS, units, DOWN_COLS), bf16),
            vmem((width // DOWN_COLS, units, DOWN_COLS), f8),
            vmem(half_scales, f32),
            vmem(half_scales, f32),
            vmem((1, width), f32),
            vmem(hadamard.shape, hadamard.dtype),
            vmem((LANES, LANES), f32),
            vmem((LANES, units), bf16),
            vmem((units, units), f8),
            vmem((1, depth), bf16),
            vmem((depth // LANES, LANES), f32),
            vmem((groups, PIECES, piece_rows, LANES), bf16),
            vmem((PIECES, 2, n, piece_rows, LANES), bf16),
            vmem((2 * n * piece_rows, LANES), f32),
            vmem((PIECES, piece_rows // 2, 4 * n, WIDE), bf16),
            vmem((2, 2 * n, units), f32),
            vmem((spans, 2, n, WIDE), bf16),
            vmem((spans, 2, n, WIDE), bf16),
            vmem((owners, held, n, LANES), bf16),
            vmem((n, held, n, LANES), bf16),
            vmem((n, held, n, LANES), bf16),
            vmem((owners, held, n, LANES), bf16),
            vmem((out_pieces, n * OUT_ROWS, LANES), f32),
            vmem((out_pieces, n, OUT_ROWS, LANES), bf16),
            vmem((out_pieces, chips, OUT_ROWS, LANES), bf16),
            vmem((out_pieces, chips, OUT_ROWS, LANES), bf16),
            vmem((out_pieces, chips, OUT_ROWS, LANES), bf16),
            dma((SLOTS,)),
            dma((5,)),
            dma((DOWN_SLOTS,)),
            dma((PIECES,)),
            dma((PIECES,)),
            dma((PIECES,)),
            dma((PIECES,)),
            dma((spans,)),
            dma((spans,)),
            dma((owners,)),
            dma((1,)),
            dma((1,)),
            dma((owners,)),
            dma((out_pieces,)),
            dma((out_pieces,)),
            dma((out_pieces,)),
            dma((out_pieces,)),
        ],
        compiler_params=pltpu.CompilerParams(
            collective_id=0, has_side_effects=True, vmem_limit_bytes=67043328
        ),
    )(
        tokens, gate_codes, gate_scales, up_codes, up_scales, down_codes, down_scales.reshape(1, width), hadamard,
    )


def fits(n, groups, tokens, gate_scales, down_codes):
    rows, depth = tokens.shape
    units, width = down_codes.shape
    scale_rows = gate_scales.shape[0]
    return (
        rows == 1
        and n == 16
        and groups == 2
        and HA % n == 0
        and units * n == HA * HB
        and HA // n <= LANES // 2
        and HB <= LANES // 2
        and HA // n % 8 == 0
        and 8 * HB % 32 == 0
        and depth == scale_rows * LANES
        and scale_rows % (groups * PIECES * 8) == 0
        and depth == 8 * groups * CHUNK
        and width == 8 * DOWN_COLS
        and units % LANES == 0
        and n // 2 <= units // LANES <= n
    )


def per_device(
    tokens, gate_codes, gate_scales, up_codes, up_scales, down_codes, down_scales, hadamard
):
    n = lax.axis_size("hx")
    groups = lax.axis_size("groups")
    if fits(n, groups, tokens, gate_scales, down_codes):
        return fused(
            n, groups, tokens, gate_codes, gate_scales, up_codes, up_scales, down_codes, down_scales, hadamard
        )
    gate_weight = dequantize(gate_codes, gate_scales)
    up_weight = dequantize(up_codes, up_scales)
    tile_rows = lax.all_gather(tokens, "hx", axis=0, tiled=True)
    gate = jnp.dot(tile_rows, gate_weight, preferred_element_type=jnp.float32)
    up_part = jnp.dot(tile_rows, up_weight, preferred_element_type=jnp.float32)
    hidden = jax.nn.silu(gate) * up_part
    factor = hadamard.astype(jnp.float32)
    gathered = lax.all_to_all(
        hidden.astype(jnp.bfloat16), "hx", split_axis=0, concat_axis=1, tiled=True
    ).astype(hidden.dtype)
    row_count = gathered.shape[0]
    cube = gathered.reshape(row_count, HA, HB)
    cube = jnp.einsum("tab,ac->tcb", cube, sylvester(HA), precision=lax.Precision.HIGHEST)
    cube = jnp.einsum("tcb,bd->tcd", cube, factor, precision=lax.Precision.HIGHEST)
    turned = lax.all_to_all(
        cube.reshape(row_count, FF).astype(jnp.bfloat16),
        "hx",
        split_axis=1,
        concat_axis=0,
        tiled=True,
    ).astype(jnp.float32)
    rotated = (turned * (1.0 / math.sqrt(FF))).astype(jnp.bfloat16)
    summed = lax.psum_scatter(
        jnp.dot(rotated, down_codes, preferred_element_type=jnp.float32),
        "hx",
        scatter_dimension=0,
        tiled=True,
    )
    mixed = (summed * down_scales[None, :]).astype(jnp.bfloat16)
    return mixed


def solution(mesh):
    in_specs = (
        P(("groups", "hx"), None),
        P(None, "hx"),
        P(None, "hx"),
        P(None, "hx"),
        P(None, "hx"),
        P("hx", None),
        P(),
        P(),
    )
    out_specs = P(("groups", "hx"), None)
    return jax.shard_map(
        per_device, mesh=mesh, in_specs=in_specs, out_specs=out_specs, check_vma=False
    )
```

```python
import functools
import math

import jax
import jax.numpy as jnp
from jax import lax
from jax.experimental import pallas as pl
from jax.experimental.pallas import tpu as pltpu
from jax.sharding import PartitionSpec as P

HA = 512
HB = 52
FF = 26624


def sylvester(size):
    index_vec = jnp.arange(size, dtype=jnp.int32)
    parity = jnp.zeros((size, size), jnp.int32)
    for level in range(max(size.bit_length() - 1, 0)):
        left_bits = jnp.right_shift(index_vec[:, None], level) & 1
        right_bits = jnp.right_shift(index_vec[None, :], level) & 1
        parity = parity + left_bits * right_bits
    return (1 - 2 * (parity % 2)).astype(jnp.float32)


def dequantize(codes, scales):
    row_total, col_total = codes.shape
    group_total = scales.shape[0]
    grouped = codes.astype(jnp.float32).reshape(group_total, row_total // group_total, col_total)
    return (grouped * scales[:, None, :]).reshape(row_total, col_total).astype(jnp.bfloat16)


LANES = 128
WIDE = 2 * LANES
PIECES = 2
MERGED = 1
CHUNK = 512
SLOTS = 6
DOWN_COLS = 1024
DOWN_SLOTS = 3
BLOCK = 64
OUT_ROWS = 16


def kernel(
    n, groups, tok_ref, gate_ref, gscale_ref, up_ref, uscale_ref, down_ref, dscale_ref, had_ref,
    out_ref,
    ring, weights, dring, down, gs, us, ds, had, corner, table, local, tok_row, tok_f32, tok_out, tok, stage, lhs, acc,
    xsend, xrecv, zbuf, recv_z, rbuf, rot, begun, part, pair_out, pair_in, sums, recv_c,
    ring_sem, load_sem, down_sem, tok_ssem, tok_rsem, fwd_ssem, fwd_rsem, x_ssem, x_rsem, z_ssem, z_rsem, r_ssem, r_rsem,
    p_ssem, p_rsem, c_ssem, c_rsem,
):
    f32, bf16, f8 = jnp.float32, jnp.bfloat16, jnp.float8_e4m3fn
    mine = lax.axis_index("groups")
    me = lax.axis_index("hx")
    chips = n // 2
    chip, core = lax.div(me, 2), lax.rem(me, 2)
    units = gate_ref.shape[1]
    tiles = units // LANES
    half_rows = gate_ref.shape[0] // groups
    chunks = half_rows // CHUNK
    piece_rows = tok.shape[3]
    down_chunks = down.shape[0]
    other = lax.rem(mine + 1, groups)

    def device(group, index):
        return {"groups": group, "hx": index}

    def remote(src, dst, send_sem, recv_sem, peer):
        return pltpu.make_async_remote_copy(
            src_ref=src, dst_ref=dst, send_sem=send_sem, recv_sem=recv_sem,
            device_id=peer, device_id_type=pl.DeviceIdType.MESH,
        )

    def flip(index, mask):
        out = index
        for bit in range(mask.bit_length()):
            if mask >> bit & 1:
                out = out + (1 - 2 * lax.rem(lax.div(index, 1 << bit), 2)) * (1 << bit)
        return out

    def chip_at(step):
        return flip(chip, step)

    partner = device(mine, chip * 2 + 1 - core)
    peers = [device(mine, lax.rem(me + step, n)) for step in range(1, n)]
    across = [device(other, chip_at(step) * 2 + core) for step in range(chips)]

    def start_weights(c, slot):
        rows = pl.ds(pl.multiple_of(mine * half_rows + c * CHUNK, CHUNK), CHUNK)
        for w, src in enumerate((gate_ref, up_ref)):
            pltpu.make_async_copy(src.at[rows], ring.at[slot, w], ring_sem.at[slot]).start()

    def wait_weights(slot):
        pltpu.make_async_copy(ring.at[slot], ring.at[slot], ring_sem.at[slot]).wait()

    def down_copy(c):
        cols = pl.ds(c * DOWN_COLS, DOWN_COLS)
        return pltpu.make_async_copy(down_ref.at[:, cols], dring.at[c % DOWN_SLOTS], down_sem.at[c % DOWN_SLOTS])

    scale_rows = gs.shape[0]
    half_scales = pl.ds(pl.multiple_of(mine * scale_rows, scale_rows), scale_rows)
    loads = [
        pltpu.make_async_copy(src, dst, load_sem.at[i])
        for i, (src, dst) in enumerate(
            (
                (tok_ref, tok_row), (had_ref, had), (dscale_ref, ds),
                (gscale_ref.at[half_scales], gs), (uscale_ref.at[half_scales], us),
            )
        )
    ]

    barrier = pltpu.get_barrier_semaphore()
    for peer in peers + across:
        pl.semaphore_signal(barrier, inc=1, device_id=peer, device_id_type=pl.DeviceIdType.MESH)
    for copy in loads:
        copy.start()

    def first(c, carry):
        start_weights(c, c)
        return carry

    lax.fori_loop(0, SLOTS, first, 0)
    loads[0].wait()
    row = tok_row[...].astype(f32)
    for k in range(tok_f32.shape[0]):
        tok_f32[k : k + 1, :] = row[:, k * LANES : (k + 1) * LANES]
    for h in range(groups):
        for p in range(PIECES):
            start = (h * PIECES + p) * piece_rows
            tok_out[h, p] = tok_f32[start : start + piece_rows, :].astype(bf16)
    for p in range(PIECES):
        tok[p, core, chip] = tok_out[mine, p]
    loads[1].wait()

    half = LANES // 2
    hb = had.shape[0]
    ha = units // hb
    corner[...] = jnp.zeros_like(corner)
    corner[:hb, :hb] = had[...].astype(f32)
    left_bits = lax.broadcasted_iota(jnp.int32, (ha, ha), 0) & lax.broadcasted_iota(jnp.int32, (ha, ha), 1)
    parity = jnp.zeros((ha, ha), jnp.int32)
    for level in range(ha.bit_length() - 1):
        parity = parity ^ (jnp.right_shift(left_bits, level) & 1)
    corner[half : half + ha, half : half + ha] = (1 - 2 * parity).astype(f32)

    def digits(unit):
        high = jnp.floor((unit + 0.5) * (1.0 / hb))
        return high, unit - hb * high

    at = lax.broadcasted_iota(jnp.int32, (LANES, LANES), 0).astype(f32)
    unit = lax.broadcasted_iota(jnp.int32, (LANES, LANES), 1).astype(f32)
    parts = corner[...].astype(bf16)
    for i in range(tiles):
        high, low = digits(unit + float(i * LANES))
        pick = jnp.where((at == low) | (at == high + half), 1.0, 0.0).astype(bf16)
        table[:, i * LANES : (i + 1) * LANES] = jnp.dot(parts, pick, preferred_element_type=f32).astype(bf16)
    factors = table[...]

    def build(i, carry):
        shape = (LANES, LANES)
        unit = (lax.broadcasted_iota(jnp.int32, shape, 0) + i * LANES).astype(f32)
        at = lax.broadcasted_iota(jnp.int32, shape, 1).astype(f32)
        high, low = digits(unit)
        pick = jnp.concatenate(
            [jnp.where(at == low, 1.0, 0.0), jnp.where(at == high + half, 1.0, 0.0)], axis=0
        ).astype(bf16)
        both = jnp.dot(pick, factors, preferred_element_type=f32)
        rows = pl.ds(pl.multiple_of(i * LANES, LANES), LANES)
        local[rows, :] = (both[:LANES] * both[LANES:]).astype(f8)
        return carry

    octet = 8 * hb
    lax.fori_loop(0, -(-octet // LANES), build, 0)

    def signs(k, carry):
        rows = pl.ds(pl.multiple_of(k * 32, 32), 32)
        base = local[rows, :].astype(bf16)
        for i in range(1, ha // 8):
            to = pl.ds(pl.multiple_of(i * octet + k * 32, 32), 32)
            local[to, :] = (base * table[half + 8 * i : half + 8 * i + 1, :]).astype(f8)
        return carry

    pl.semaphore_wait(barrier, len(peers) + len(across))

    hops = [(d, step) for step in reversed(range(chips)) for d in reversed(range(groups)) if (d, step) != (0, 0)]

    def tok_send(p, d, step):
        group = lax.rem(mine + d, groups)
        return remote(
            tok_out.at[group, p], tok.at[p, core, d * chips + chip], tok_ssem.at[p], tok_rsem.at[p],
            device(group, chip_at(step) * 2 + core),
        )

    def tok_all(p):
        blocks = pl.ds(0, len(hops))
        at = tok.at[p, core, blocks]
        return remote(at, at, tok_ssem.at[p], tok_rsem.at[p], partner)

    def forward(p, which):
        return remote(tok.at[p, which], tok.at[p, which], fwd_ssem.at[p], fwd_rsem.at[p], partner)

    for p in range(PIECES):
        for d, step in hops:
            tok_send(p, d, step).start()

    lhs[...] = jnp.zeros_like(lhs)
    acc[...] = jnp.zeros_like(acc)
    lax.fori_loop(0, octet // 32, signs, 0)

    def convert(c):
        wait_weights(c % SLOTS)

        def block(k, carry):
            rows = pl.ds(pl.multiple_of(k * BLOCK, BLOCK), BLOCK)
            to = pl.ds(pl.multiple_of(c * CHUNK + k * BLOCK, BLOCK), BLOCK)
            for w in range(2):
                weights[w, to, :] = ring[c % SLOTS, w, rows, :].astype(f8)
            return carry

        lax.fori_loop(0, CHUNK // BLOCK, block, 0)
        if c + SLOTS < chunks:
            start_weights(c + SLOTS, c % SLOTS)
        elif c + SLOTS - chunks < DOWN_SLOTS:
            down_copy(c + SLOTS - chunks).start()

    def convert_down(c):
        down_copy(c).wait()

        def block(k, carry):
            rows = pl.ds(pl.multiple_of(k * BLOCK, BLOCK), BLOCK)
            down[c, rows, :] = dring[c % DOWN_SLOTS, rows, :].astype(f8)
            return carry

        lax.fori_loop(0, units // BLOCK, block, 0)
        if c + DOWN_SLOTS < down_chunks:
            down_copy(c + DOWN_SLOTS).start()

    def relay(p):
        tok_all(p).wait_recv()
        forward(p, core).start()

    def ready(p):
        forward(p, 1 - core).wait_recv()
        stage[...] = tok[p].reshape(stage.shape).astype(f32)
        for k in range(piece_rows):
            part_rows = [
                stage[pl.ds(w * n * piece_rows + k, n, stride=piece_rows), :] for w in range(2)
            ]
            both = jnp.concatenate(
                [part_rows[0][:chips], part_rows[1][:chips], part_rows[0][chips:], part_rows[1][chips:]], axis=0
            ).astype(bf16)
            q, odd = divmod(k, 2)
            lhs[p, q, odd * 2 * n : (odd + 1) * 2 * n, odd * LANES : (odd + 1) * LANES] = both

    def products(p, cols, tail):
        sums_now = [None, None]
        for q in range(piece_rows // 2):
            left = lhs[p, q]
            row = p * piece_rows + 2 * q
            rows = slice(row * LANES, (row + 2) * LANES)
            if tail:
                right = jnp.concatenate([weights[0, rows, cols], weights[1, rows, cols]], axis=1)
                scale = jnp.concatenate([gs[row : row + 2, cols], us[row : row + 2, cols]], axis=1)
                sides = [(right, scale)]
            else:
                sides = [(weights[w, rows, cols], scale[row : row + 2, cols]) for w, scale in ((0, gs), (1, us))]
            for w, (right, scale) in enumerate(sides):
                res = jnp.dot(left, right, preferred_element_type=f32)
                new = res[: 2 * n] * scale[0:1, :] + res[2 * n :] * scale[1:2, :]
                sums_now[w] = new if sums_now[w] is None else sums_now[w] + new
        if tail:
            width = sums_now[0].shape[1] // 2
            return sums_now[0][:, :width], sums_now[0][:, width:]
        return sums_now

    spans = [(at, min(WIDE, units - at)) for at in range(0, units, WIDE)]

    def x_send(j, width):
        at = (j, slice(None), slice(None), pl.ds(0, width))
        return remote(xsend.at[at], xrecv.at[at], x_ssem.at[j], x_rsem.at[j], across[0])

    def run(pieces):
        final = pieces[-1] + 1 == PIECES
        for j, (at, width) in enumerate(spans):
            cols = slice(at, at + width)
            pair = None
            for p in pieces:
                new = products(p, cols, width < WIDE)
                pair = new if pair is None else [a + b for a, b in zip(pair, new)]
            for w in range(2):
                if not final:
                    acc[w, :, cols] += pair[w]
                else:
                    total = acc[w, :, cols] + pair[w]
                    acc[w, :n, cols] = total[:n]
                    xsend[j, w, :, :width] = total[n:].astype(bf16)
            if final:
                x_send(j, width).start()

    for copy in loads[2:]:
        copy.wait()
    per_piece = chunks // PIECES
    last = PIECES - MERGED
    early = chunks - per_piece
    for c in range(early):
        convert(c)
    relay(0)
    convert(early)
    relay(1)
    for p in range(PIECES):
        ready(p)
        if p < last:
            run([p])
        if p + 2 < PIECES:
            relay(p + 2)
        if p == 0:
            for c in range(early + 1, chunks):
                convert(c)
    run(list(range(last, PIECES)))

    for c in range(3):
        convert_down(c)
    turned = None
    for j, (at, width) in enumerate(spans):
        x_send(j, width).wait_recv()
        cols = slice(at, at + width)
        gate = acc[0, :n, cols] + xrecv[j, 0, :, :width].astype(f32)
        lift = acc[1, :n, cols] + xrecv[j, 1, :, :width].astype(f32)
        hidden = (gate / (1.0 + jnp.exp(-gate)) * lift).astype(bf16)
        new = jnp.dot(hidden, local[cols, :], preferred_element_type=f32)
        turned = new if turned is None else turned + new
    turned = turned.astype(bf16)

    owners = zbuf.shape[0]
    quarter = n // 4

    def owner_at(o):
        return quarter + (o % 2) * quarter + o // 2

    def held(o):
        return len(range(o, tiles, owners))

    for j in range(tiles):
        zbuf[j % owners, j // owners] = turned[:, j * LANES : (j + 1) * LANES]

    def z_out(o):
        count = pl.ds(0, held(o))
        return remote(
            zbuf.at[o, count], recv_z.at[me, count], z_ssem.at[o], z_rsem.at[0], device(mine, owner_at(o))
        )

    for o in range(owners):

        @pl.when(me != owner_at(o))
        def _():
            z_out(o).start()

        @pl.when(me == owner_at(o))
        def _():
            recv_z[me] = zbuf[o]

    for c in range(3, 6):
        convert_down(c)

    place = me - quarter
    number = lax.rem(place, quarter) * 2 + lax.div(place, quarter)
    owns = jnp.logical_and(me >= quarter, me < 3 * quarter)
    extra = tiles % owners
    scale = 1.0 / math.sqrt(units * n)

    def r_out(i, count):
        at = pl.ds(0, count)
        peer = flip(me, i)
        return remote(rbuf.at[peer, at], rot.at[number, at], r_ssem.at[0], r_rsem.at[number], device(mine, peer))

    def turn(count):
        at = pl.ds(0, count)
        every = recv_z.at[pl.ds(0, n - 1), at]
        remote(every, every, z_ssem.at[0], z_rsem.at[0], partner).wait_recv()
        for t in range(count):
            cube = [recv_z[h, t].astype(f32) for h in range(n)]
            span = 1
            while span < n:
                nxt = list(cube)
                for h in range(n):
                    if h & span == 0:
                        nxt[h] = cube[h] + cube[h | span]
                        nxt[h | span] = cube[h] - cube[h | span]
                cube = nxt
                span *= 2
            for h in range(n):
                rbuf[h, t] = (cube[h] * scale).astype(bf16)
        for i in reversed(range(1, n)):
            r_out(i, count).start()
        rot[number] = rbuf[me]

    many, few = held(0), held(owners - 1)

    def by_count(action):
        if extra == 0:
            pl.when(owns)(lambda: action(many))
        else:
            pl.when(jnp.logical_and(owns, number < extra))(lambda: action(many))
            pl.when(jnp.logical_and(owns, number >= extra))(lambda: action(few))

    by_count(turn)

    for c in range(6, down_chunks):
        convert_down(c)

    def arrived(parity):
        for o in range(parity, owners, 2):

            @pl.when(me != owner_at(o))
            def _(o=o):
                count = pl.ds(0, held(o))
                remote(
                    rbuf.at[0, count], rot.at[o, count], r_ssem.at[0], r_rsem.at[o], device(mine, owner_at(o))
                ).wait_recv()

    side = lax.div(me, n // 2)
    even = [(o, k) for k in range(rot.shape[1]) for o in range(0, owners, 2) if o + k * owners < tiles]
    common = [(o, k) for o, k in even if o + 1 + k * owners < tiles]
    single = [(o, k) for o, k in even if (o, k) not in common]

    def operands(parity, pairs):
        left = [rot[o + parity, k] for o, k in pairs]
        rows = [pl.ds(pl.multiple_of((o + k * owners + parity) * LANES, LANES), LANES) for o, k in pairs]
        return left, rows

    def product(c, left, rows):
        right = jnp.concatenate([down[c, at, :] for at in rows], axis=0)
        return jnp.dot(jnp.concatenate(left, axis=1), right, preferred_element_type=f32)

    pl.when(side == 0)(lambda: arrived(0))
    pl.when(side == 1)(lambda: arrived(1))
    left, rows = operands(side, common)
    for c in range(down_chunks):
        begun[c] = product(c, left, rows)
    pl.when(side == 0)(lambda: arrived(1))
    pl.when(side == 1)(lambda: arrived(0))
    left, rows = operands(1 - side, common)
    more, more_rows = operands(0, single)
    left, rows = left + more, rows + more_rows

    out_pieces = recv_c.shape[0]
    per_out = down_chunks // out_pieces
    blocks = DOWN_COLS // LANES
    own_rows = chips * OUT_ROWS

    def pair_copy(p, which):
        at = pl.ds(which * chips, chips)
        return remote(pair_out.at[p, at], pair_in.at[p], p_ssem.at[p], p_rsem.at[p], partner)

    def c_out(p, step):
        to = chip_at(step)
        return remote(
            sums.at[p, to], recv_c.at[p, chip], c_ssem.at[p], c_rsem.at[p], device(mine, to * 2 + core)
        )

    def c_all(p, ref):
        at = ref.at[p, pl.ds(0, chips - 1)]
        return remote(at, at, c_ssem.at[p], c_rsem.at[p], partner)

    def finish(p):
        pair_copy(p, core).wait_recv()
        rows = pl.ds(pl.multiple_of(core * own_rows, own_rows), own_rows)
        both = part[p, rows, :] + pair_in[p].reshape(own_rows, LANES).astype(f32)
        sums[p] = both.astype(bf16).reshape(chips, OUT_ROWS, LANES)
        for step in reversed(range(1, chips)):
            c_out(p, step).start()
        recv_c[p, chip] = sums[p, chip]

    for p in range(out_pieces):
        for k in range(per_out):
            res = begun[p * per_out + k] + product(p * per_out + k, left, rows)
            for b in range(blocks):
                part[p, pl.ds(k * blocks + b, n, stride=OUT_ROWS), :] = res[:, b * LANES : (b + 1) * LANES]
        pair_out[p] = part[p].astype(bf16).reshape(n, OUT_ROWS, LANES)
        pair_copy(p, 1 - core).start()
        if p > 0:
            finish(p - 1)
    finish(out_pieces - 1)

    for p in range(out_pieces):
        c_all(p, recv_c).wait_recv()
        total = recv_c[p, 0].astype(f32)
        for h in range(1, chips):
            total = total + recv_c[p, h].astype(f32)
        for r in range(OUT_ROWS):
            cols = slice((p * OUT_ROWS + r) * LANES, (p * OUT_ROWS + r + 1) * LANES)
            out_ref[:, cols] = (total[r : r + 1, :] * ds[:, cols]).astype(out_ref.dtype)

    for p in range(PIECES):
        tok_all(p).wait_send()
        forward(p, core).wait_send()
    for j, (at, width) in enumerate(spans):
        x_send(j, width).wait_send()
    for o in range(owners):

        @pl.when(me != owner_at(o))
        def _():
            z_out(o).wait_send()

    def drain(count):
        every = rbuf.at[pl.ds(0, n - 1), pl.ds(0, count)]
        remote(every, every, r_ssem.at[0], r_rsem.at[0], partner).wait_send()

    by_count(drain)
    for p in range(out_pieces):
        pair_copy(p, 1 - core).wait_send()
        c_all(p, sums).wait_send()


def fused(n, groups, tokens, gate_codes, gate_scales, up_codes, up_scales, down_codes, down_scales, hadamard):
    depth, units = gate_codes.shape
    width = down_codes.shape[1]
    tiles = units // LANES
    piece_rows = depth // (groups * PIECES * LANES)
    half_scales = (gate_scales.shape[0] // groups, units)
    out_pieces = width // (LANES * OUT_ROWS)
    owners = n // 2
    held = -(-tiles // owners)
    spans = -(-units // WIDE)
    chips = n // 2
    bf16, f32, f8 = jnp.bfloat16, jnp.float32, jnp.float8_e4m3fn
    dma = pltpu.SemaphoreType.DMA
    vmem = pltpu.VMEM
    return pl.pallas_call(
        functools.partial(kernel, n, groups),
        out_shape=jax.ShapeDtypeStruct((1, width), bf16),
        in_specs=[pl.BlockSpec(memory_space=pl.ANY)] * 8,
        out_specs=pl.BlockSpec(memory_space=pltpu.VMEM),
        scratch_shapes=[
            vmem((SLOTS, 2, CHUNK, units), bf16),
            vmem((2, depth // groups, units), f8),
            vmem((DOWN_SLOTS, units, DOWN_COLS), bf16),
            vmem((width // DOWN_COLS, units, DOWN_COLS), f8),
            vmem(half_scales, f32),
            vmem(half_scales, f32),
            vmem((1, width), f32),
            vmem(hadamard.shape, hadamard.dtype),
            vmem((LANES, LANES), f32),
            vmem((LANES, units), bf16),
            vmem((units, units), f8),
            vmem((1, depth), bf16),
            vmem((depth // LANES, LANES), f32),
            vmem((groups, PIECES, piece_rows, LANES), bf16),
            vmem((PIECES, 2, n, piece_rows, LANES), bf16),
            vmem((2 * n * piece_rows, LANES), f32),
            vmem((PIECES, piece_rows // 2, 4 * n, WIDE), bf16),
            vmem((2, 2 * n, units), f32),
            vmem((spans, 2, n, WIDE), bf16),
            vmem((spans, 2, n, WIDE), bf16),
            vmem((owners, held, n, LANES), bf16),
            vmem((n, held, n, LANES), bf16),
            vmem((n, held, n, LANES), bf16),
            vmem((owners, held, n, LANES), bf16),
            vmem((width // DOWN_COLS, n, DOWN_COLS), f32),
            vmem((out_pieces, n * OUT_ROWS, LANES), f32),
            vmem((out_pieces, n, OUT_ROWS, LANES), bf16),
            vmem((out_pieces, chips, OUT_ROWS, LANES), bf16),
            vmem((out_pieces, chips, OUT_ROWS, LANES), bf16),
            vmem((out_pieces, chips, OUT_ROWS, LANES), bf16),
            dma((SLOTS,)),
            dma((5,)),
            dma((DOWN_SLOTS,)),
            dma((PIECES,)),
            dma((PIECES,)),
            dma((PIECES,)),
            dma((PIECES,)),
            dma((spans,)),
            dma((spans,)),
            dma((owners,)),
            dma((1,)),
            dma((1,)),
            dma((owners,)),
            dma((out_pieces,)),
            dma((out_pieces,)),
            dma((out_pieces,)),
            dma((out_pieces,)),
        ],
        compiler_params=pltpu.CompilerParams(
            collective_id=0, has_side_effects=True, vmem_limit_bytes=67043328
        ),
    )(
        tokens, gate_codes, gate_scales, up_codes, up_scales, down_codes, down_scales.reshape(1, width), hadamard,
    )


def fits(n, groups, tokens, gate_scales, down_codes):
    rows, depth = tokens.shape
    units, width = down_codes.shape
    scale_rows = gate_scales.shape[0]
    return (
        rows == 1
        and n == 16
        and groups == 2
        and HA % n == 0
        and units * n == HA * HB
        and HA // n <= LANES // 2
        and HB <= LANES // 2
        and HA // n % 8 == 0
        and 8 * HB % 32 == 0
        and depth == scale_rows * LANES
        and scale_rows % (groups * PIECES * 8) == 0
        and depth == 8 * groups * CHUNK
        and width == 8 * DOWN_COLS
        and units % LANES == 0
        and n // 2 <= units // LANES <= n
    )


def per_device(
    tokens, gate_codes, gate_scales, up_codes, up_scales, down_codes, down_scales, hadamard
):
    n = lax.axis_size("hx")
    groups = lax.axis_size("groups")
    if fits(n, groups, tokens, gate_scales, down_codes):
        return fused(
            n, groups, tokens, gate_codes, gate_scales, up_codes, up_scales, down_codes, down_scales, hadamard
        )
    gate_weight = dequantize(gate_codes, gate_scales)
    up_weight = dequantize(up_codes, up_scales)
    tile_rows = lax.all_gather(tokens, "hx", axis=0, tiled=True)
    gate = jnp.dot(tile_rows, gate_weight, preferred_element_type=jnp.float32)
    up_part = jnp.dot(tile_rows, up_weight, preferred_element_type=jnp.float32)
    hidden = jax.nn.silu(gate) * up_part
    factor = hadamard.astype(jnp.float32)
    gathered = lax.all_to_all(
        hidden.astype(jnp.bfloat16), "hx", split_axis=0, concat_axis=1, tiled=True
    ).astype(hidden.dtype)
    row_count = gathered.shape[0]
    cube = gathered.reshape(row_count, HA, HB)
    cube = jnp.einsum("tab,ac->tcb", cube, sylvester(HA), precision=lax.Precision.HIGHEST)
    cube = jnp.einsum("tcb,bd->tcd", cube, factor, precision=lax.Precision.HIGHEST)
    turned = lax.all_to_all(
        cube.reshape(row_count, FF).astype(jnp.bfloat16),
        "hx",
        split_axis=1,
        concat_axis=0,
        tiled=True,
    ).astype(jnp.float32)
    rotated = (turned * (1.0 / math.sqrt(FF))).astype(jnp.bfloat16)
    summed = lax.psum_scatter(
        jnp.dot(rotated, down_codes, preferred_element_type=jnp.float32),
        "hx",
        scatter_dimension=0,
        tiled=True,
    )
    mixed = (summed * down_scales[None, :]).astype(jnp.bfloat16)
    return mixed


def solution(mesh):
    in_specs = (
        P(("groups", "hx"), None),
        P(None, "hx"),
        P(None, "hx"),
        P(None, "hx"),
        P(None, "hx"),
        P("hx", None),
        P(),
        P(),
    )
    out_specs = P(("groups", "hx"), None)
    return jax.shard_map(
        per_device, mesh=mesh, in_specs=in_specs, out_specs=out_specs, check_vma=False
    )
```

```python
import functools
import math

import jax
import jax.numpy as jnp
from jax import lax
from jax.experimental import pallas as pl
from jax.experimental.pallas import tpu as pltpu
from jax.sharding import PartitionSpec as P

HA = 512
HB = 52
FF = 26624


def sylvester(size):
    index_vec = jnp.arange(size, dtype=jnp.int32)
    parity = jnp.zeros((size, size), jnp.int32)
    for level in range(max(size.bit_length() - 1, 0)):
        left_bits = jnp.right_shift(index_vec[:, None], level) & 1
        right_bits = jnp.right_shift(index_vec[None, :], level) & 1
        parity = parity + left_bits * right_bits
    return (1 - 2 * (parity % 2)).astype(jnp.float32)


def dequantize(codes, scales):
    row_total, col_total = codes.shape
    group_total = scales.shape[0]
    grouped = codes.astype(jnp.float32).reshape(group_total, row_total // group_total, col_total)
    return (grouped * scales[:, None, :]).reshape(row_total, col_total).astype(jnp.bfloat16)


LANES = 128
WIDE = 2 * LANES
PIECES = 2
CHUNK = 512
SLOTS = 6
DOWN_COLS = 1024
DOWN_SLOTS = 3
BLOCK = 64
PARTS = (4, 4)


def kernel(
    n, groups, tok_ref, gate_ref, gscale_ref, up_ref, uscale_ref, down_ref, dscale_ref, had_ref,
    out_ref,
    ring, weights, dring, down, gs, us, ds, had, corner, table, local, tok_row, tok_f32, tok_out, tok, stage, lhs, acc,
    xsend, xrecv, zbuf, recv_z, rbuf, rot, begun, part, pair_out, pair_in, sums, recv_c,
    ring_sem, load_sem, down_sem, tok_ssem, tok_rsem, fwd_ssem, fwd_rsem, x_ssem, x_rsem, z_ssem, z_rsem, r_ssem, r_rsem,
    p_ssem, p_rsem, c_ssem, c_rsem,
):
    f32, bf16, f8 = jnp.float32, jnp.bfloat16, jnp.float8_e4m3fn
    mine = lax.axis_index("groups")
    me = lax.axis_index("hx")
    chips = n // 2
    chip, core = lax.div(me, 2), lax.rem(me, 2)
    units = gate_ref.shape[1]
    tiles = units // LANES
    half_rows = gate_ref.shape[0] // groups
    chunks = half_rows // CHUNK
    piece_rows = tok.shape[3]
    down_chunks = down.shape[0]
    other = lax.rem(mine + 1, groups)

    def device(group, index):
        return {"groups": group, "hx": index}

    def remote(src, dst, send_sem, recv_sem, peer):
        return pltpu.make_async_remote_copy(
            src_ref=src, dst_ref=dst, send_sem=send_sem, recv_sem=recv_sem,
            device_id=peer, device_id_type=pl.DeviceIdType.MESH,
        )

    def flip(index, mask):
        out = index
        for bit in range(mask.bit_length()):
            if mask >> bit & 1:
                out = out + (1 - 2 * lax.rem(lax.div(index, 1 << bit), 2)) * (1 << bit)
        return out

    def chip_at(step):
        return flip(chip, step)

    partner = device(mine, chip * 2 + 1 - core)
    peers = [device(mine, lax.rem(me + step, n)) for step in range(1, n)]
    across = [device(other, chip_at(step) * 2 + core) for step in range(chips)]

    def start_weights(c, slot):
        rows = pl.ds(pl.multiple_of(mine * half_rows + c * CHUNK, CHUNK), CHUNK)
        for w, src in enumerate((gate_ref, up_ref)):
            pltpu.make_async_copy(src.at[rows], ring.at[slot, w], ring_sem.at[slot]).start()

    def wait_weights(slot):
        pltpu.make_async_copy(ring.at[slot], ring.at[slot], ring_sem.at[slot]).wait()

    def down_copy(c):
        cols = pl.ds(c * DOWN_COLS, DOWN_COLS)
        return pltpu.make_async_copy(down_ref.at[:, cols], dring.at[c % DOWN_SLOTS], down_sem.at[c % DOWN_SLOTS])

    scale_rows = gs.shape[0]
    half_scales = pl.ds(pl.multiple_of(mine * scale_rows, scale_rows), scale_rows)
    loads = [
        pltpu.make_async_copy(src, dst, load_sem.at[i])
        for i, (src, dst) in enumerate(
            (
                (tok_ref, tok_row), (had_ref, had), (dscale_ref, ds),
                (gscale_ref.at[half_scales], gs), (uscale_ref.at[half_scales], us),
            )
        )
    ]

    barrier = pltpu.get_barrier_semaphore()
    for peer in peers + across:
        pl.semaphore_signal(barrier, inc=1, device_id=peer, device_id_type=pl.DeviceIdType.MESH)
    for copy in loads:
        copy.start()

    def first(c, carry):
        start_weights(c, c)
        return carry

    lax.fori_loop(0, SLOTS, first, 0)
    loads[0].wait()
    row = tok_row[...].astype(f32)
    for k in range(tok_f32.shape[0]):
        tok_f32[k : k + 1, :] = row[:, k * LANES : (k + 1) * LANES]
    for h in range(groups):
        for p in range(PIECES):
            start = (h * PIECES + p) * piece_rows
            tok_out[h, p] = tok_f32[start : start + piece_rows, :].astype(bf16)
    for p in range(PIECES):
        tok[p, core, chip] = tok_out[mine, p]
    loads[1].wait()

    half = LANES // 2
    hb = had.shape[0]
    ha = units // hb
    corner[...] = jnp.zeros_like(corner)
    corner[:hb, :hb] = had[...].astype(f32)
    left_bits = lax.broadcasted_iota(jnp.int32, (ha, ha), 0) & lax.broadcasted_iota(jnp.int32, (ha, ha), 1)
    parity = jnp.zeros((ha, ha), jnp.int32)
    for level in range(ha.bit_length() - 1):
        parity = parity ^ (jnp.right_shift(left_bits, level) & 1)
    corner[half : half + ha, half : half + ha] = (1 - 2 * parity).astype(f32)

    def digits(unit):
        high = jnp.floor((unit + 0.5) * (1.0 / hb))
        return high, unit - hb * high

    at = lax.broadcasted_iota(jnp.int32, (LANES, LANES), 0).astype(f32)
    unit = lax.broadcasted_iota(jnp.int32, (LANES, LANES), 1).astype(f32)
    parts = corner[...].astype(bf16)
    for i in range(tiles):
        high, low = digits(unit + float(i * LANES))
        pick = jnp.where((at == low) | (at == high + half), 1.0, 0.0).astype(bf16)
        table[:, i * LANES : (i + 1) * LANES] = jnp.dot(parts, pick, preferred_element_type=f32).astype(bf16)
    factors = table[...]

    def build(i, carry):
        shape = (LANES, LANES)
        unit = (lax.broadcasted_iota(jnp.int32, shape, 0) + i * LANES).astype(f32)
        at = lax.broadcasted_iota(jnp.int32, shape, 1).astype(f32)
        high, low = digits(unit)
        pick = jnp.concatenate(
            [jnp.where(at == low, 1.0, 0.0), jnp.where(at == high + half, 1.0, 0.0)], axis=0
        ).astype(bf16)
        both = jnp.dot(pick, factors, preferred_element_type=f32)
        rows = pl.ds(pl.multiple_of(i * LANES, LANES), LANES)
        local[rows, :] = (both[:LANES] * both[LANES:]).astype(f8)
        return carry

    octet = 8 * hb
    lax.fori_loop(0, -(-octet // LANES), build, 0)

    def signs(k, carry):
        rows = pl.ds(pl.multiple_of(k * 32, 32), 32)
        base = local[rows, :].astype(bf16)
        for i in range(1, ha // 8):
            to = pl.ds(pl.multiple_of(i * octet + k * 32, 32), 32)
            local[to, :] = (base * table[half + 8 * i : half + 8 * i + 1, :]).astype(f8)
        return carry

    pl.semaphore_wait(barrier, len(peers) + len(across))

    hops = [(d, step) for step in reversed(range(chips)) for d in reversed(range(groups)) if (d, step) != (0, 0)]

    def tok_send(p, d, step):
        group = lax.rem(mine + d, groups)
        return remote(
            tok_out.at[group, p], tok.at[p, core, d * chips + chip], tok_ssem.at[p], tok_rsem.at[p],
            device(group, chip_at(step) * 2 + core),
        )

    def tok_all(p):
        blocks = pl.ds(0, len(hops))
        at = tok.at[p, core, blocks]
        return remote(at, at, tok_ssem.at[p], tok_rsem.at[p], partner)

    def forward(p, which):
        return remote(tok.at[p, which], tok.at[p, which], fwd_ssem.at[p], fwd_rsem.at[p], partner)

    for p in range(PIECES):
        for d, step in hops:
            tok_send(p, d, step).start()

    lhs[...] = jnp.zeros_like(lhs)
    acc[...] = jnp.zeros_like(acc)
    lax.fori_loop(0, octet // 32, signs, 0)

    def convert(c):
        wait_weights(c % SLOTS)

        def block(k, carry):
            rows = pl.ds(pl.multiple_of(k * BLOCK, BLOCK), BLOCK)
            to = pl.ds(pl.multiple_of(c * CHUNK + k * BLOCK, BLOCK), BLOCK)
            for w in range(2):
                weights[w, to, :] = ring[c % SLOTS, w, rows, :].astype(f8)
            return carry

        lax.fori_loop(0, CHUNK // BLOCK, block, 0)
        if c + SLOTS < chunks:
            start_weights(c + SLOTS, c % SLOTS)
        elif c + SLOTS - chunks < DOWN_SLOTS:
            down_copy(c + SLOTS - chunks).start()

    def convert_down(c):
        down_copy(c).wait()

        def block(k, carry):
            rows = pl.ds(pl.multiple_of(k * BLOCK, BLOCK), BLOCK)
            down[c, rows, :] = dring[c % DOWN_SLOTS, rows, :].astype(f8)
            return carry

        lax.fori_loop(0, units // BLOCK, block, 0)
        if c + DOWN_SLOTS < down_chunks:
            down_copy(c + DOWN_SLOTS).start()

    def relay(p):
        tok_all(p).wait_recv()
        forward(p, core).start()

    def ready(p):
        forward(p, 1 - core).wait_recv()
        stage[...] = tok[p].reshape(stage.shape).astype(f32)
        for k in range(piece_rows):
            part_rows = [
                stage[pl.ds(w * n * piece_rows + k, n, stride=piece_rows), :] for w in range(2)
            ]
            both = jnp.concatenate(
                [part_rows[0][:chips], part_rows[1][:chips], part_rows[0][chips:], part_rows[1][chips:]], axis=0
            ).astype(bf16)
            q, odd = divmod(k, 2)
            lhs[p, q, odd * 2 * n : (odd + 1) * 2 * n, odd * LANES : (odd + 1) * LANES] = both

    def products(p, cols, tail):
        sums_now = [None, None]
        for q in range(piece_rows // 2):
            left = lhs[p, q]
            row = p * piece_rows + 2 * q
            rows = slice(row * LANES, (row + 2) * LANES)
            if tail:
                right = jnp.concatenate([weights[0, rows, cols], weights[1, rows, cols]], axis=1)
                scale = jnp.concatenate([gs[row : row + 2, cols], us[row : row + 2, cols]], axis=1)
                sides = [(right, scale)]
            else:
                sides = [(weights[w, rows, cols], scale[row : row + 2, cols]) for w, scale in ((0, gs), (1, us))]
            for w, (right, scale) in enumerate(sides):
                res = jnp.dot(left, right, preferred_element_type=f32)
                new = res[: 2 * n] * scale[0:1, :] + res[2 * n :] * scale[1:2, :]
                sums_now[w] = new if sums_now[w] is None else sums_now[w] + new
        if tail:
            width = sums_now[0].shape[1] // 2
            return sums_now[0][:, :width], sums_now[0][:, width:]
        return sums_now

    spans = [(at, min(WIDE, units - at)) for at in range(0, units, WIDE)]

    def x_send(j, width):
        at = (j, slice(None), slice(None), pl.ds(0, width))
        return remote(xsend.at[at], xrecv.at[at], x_ssem.at[j], x_rsem.at[j], across[0])

    def run(pieces):
        final = pieces[-1] + 1 == PIECES
        for j, (at, width) in enumerate(spans):
            cols = slice(at, at + width)
            pair = None
            for p in pieces:
                new = products(p, cols, width < WIDE)
                pair = new if pair is None else [a + b for a, b in zip(pair, new)]
            for w in range(2):
                if not final:
                    acc[w, :, cols] += pair[w]
                else:
                    total = acc[w, :, cols] + pair[w]
                    acc[w, :n, cols] = total[:n]
                    xsend[j, w, :, :width] = total[n:].astype(bf16)
            if final:
                x_send(j, width).start()

    for copy in loads[2:]:
        copy.wait()
    early = chunks // PIECES

    def convert_more():
        for c in range(early, SLOTS):
            convert(c)

    for c in range(early):
        convert(c)
    pl.when(me < 3 * n // 4)(convert_more)
    relay(0)
    relay(1)
    pl.when(me >= 3 * n // 4)(convert_more)
    ready(0)
    run([0])
    for c in range(SLOTS, chunks):
        convert(c)
    ready(1)
    run([1])

    for c in range(3):
        convert_down(c)
    turned = None
    for j, (at, width) in enumerate(spans):
        x_send(j, width).wait_recv()
        cols = slice(at, at + width)
        gate = acc[0, :n, cols] + xrecv[j, 0, :, :width].astype(f32)
        lift = acc[1, :n, cols] + xrecv[j, 1, :, :width].astype(f32)
        hidden = (gate / (1.0 + jnp.exp(-gate)) * lift).astype(bf16)
        new = jnp.dot(hidden, local[cols, :], preferred_element_type=f32)
        turned = new if turned is None else turned + new
    turned = turned.astype(bf16)

    owners = zbuf.shape[0]
    quarter = n // 4

    def owner_at(o):
        return quarter + (o % 2) * quarter + o // 2

    def held(o):
        return len(range(o, tiles, owners))

    for j in range(tiles):
        zbuf[j % owners, j // owners] = turned[:, j * LANES : (j + 1) * LANES]

    def z_out(o):
        count = pl.ds(0, held(o))
        return remote(
            zbuf.at[o, count], recv_z.at[me, count], z_ssem.at[o], z_rsem.at[0], device(mine, owner_at(o))
        )

    for o in range(owners):

        @pl.when(me != owner_at(o))
        def _():
            z_out(o).start()

        @pl.when(me == owner_at(o))
        def _():
            recv_z[me] = zbuf[o]

    for c in range(3, 6):
        convert_down(c)

    place = me - quarter
    number = lax.rem(place, quarter) * 2 + lax.div(place, quarter)
    owns = jnp.logical_and(me >= quarter, me < 3 * quarter)
    extra = tiles % owners
    scale = 1.0 / math.sqrt(units * n)

    def r_out(i, count):
        at = pl.ds(0, count)
        peer = flip(me, i)
        return remote(rbuf.at[peer, at], rot.at[number, at], r_ssem.at[0], r_rsem.at[number], device(mine, peer))

    def turn(count):
        at = pl.ds(0, count)
        every = recv_z.at[pl.ds(0, n - 1), at]
        remote(every, every, z_ssem.at[0], z_rsem.at[0], partner).wait_recv()
        for t in range(count):
            cube = [recv_z[h, t].astype(f32) for h in range(n)]
            span = 1
            while span < n:
                nxt = list(cube)
                for h in range(n):
                    if h & span == 0:
                        nxt[h] = cube[h] + cube[h | span]
                        nxt[h | span] = cube[h] - cube[h | span]
                cube = nxt
                span *= 2
            for h in range(n):
                rbuf[h, t] = (cube[h] * scale).astype(bf16)
        for i in reversed(range(1, n)):
            r_out(i, count).start()
        rot[number] = rbuf[me]

    many, few = held(0), held(owners - 1)

    def by_count(action):
        if extra == 0:
            pl.when(owns)(lambda: action(many))
        else:
            pl.when(jnp.logical_and(owns, number < extra))(lambda: action(many))
            pl.when(jnp.logical_and(owns, number >= extra))(lambda: action(few))

    by_count(turn)

    for c in range(6, down_chunks):
        convert_down(c)

    def arrived(parity):
        for o in range(parity, owners, 2):

            @pl.when(me != owner_at(o))
            def _(o=o):
                count = pl.ds(0, held(o))
                remote(
                    rbuf.at[0, count], rot.at[o, count], r_ssem.at[0], r_rsem.at[o], device(mine, owner_at(o))
                ).wait_recv()

    side = lax.div(me, n // 2)
    even = [(o, k) for k in range(rot.shape[1]) for o in range(0, owners, 2) if o + k * owners < tiles]
    common = [(o, k) for o, k in even if o + 1 + k * owners < tiles]
    single = [(o, k) for o, k in even if (o, k) not in common]

    def operands(parity, pairs):
        left = [rot[o + parity, k] for o, k in pairs]
        rows = [pl.ds(pl.multiple_of((o + k * owners + parity) * LANES, LANES), LANES) for o, k in pairs]
        return left, rows

    def product(c, left, rows):
        right = jnp.concatenate([down[c, at, :] for at in rows], axis=0)
        return jnp.dot(jnp.concatenate(left, axis=1), right, preferred_element_type=f32)

    pl.when(side == 0)(lambda: arrived(0))
    pl.when(side == 1)(lambda: arrived(1))
    left, rows = operands(side, common)
    for c in range(down_chunks):
        begun[c] = product(c, left, rows)
    pl.when(side == 0)(lambda: arrived(1))
    pl.when(side == 1)(lambda: arrived(0))
    left, rows = operands(1 - side, common)
    more, more_rows = operands(0, single)
    left, rows = left + more, rows + more_rows

    blocks = DOWN_COLS // LANES
    starts = [sum(PARTS[:p]) for p in range(len(PARTS))]
    own_rows = [chips * size * blocks for size in PARTS]

    def pair_copy(p, which):
        at = pl.ds(which * chips, chips)
        return remote(pair_out[p].at[at], pair_in[p], p_ssem.at[p], p_rsem.at[p], partner)

    def c_out(p, step):
        to = chip_at(step)
        return remote(
            sums[p].at[to], recv_c[p].at[chip], c_ssem.at[p], c_rsem.at[p], device(mine, to * 2 + core)
        )

    def c_all(p, ref):
        at = ref.at[pl.ds(0, chips - 1)]
        return remote(at, at, c_ssem.at[p], c_rsem.at[p], partner)

    def finish(p):
        pair_copy(p, core).wait_recv()
        rows = pl.ds(pl.multiple_of(core * own_rows[p], own_rows[p]), own_rows[p])
        both = part[p][rows, :] + pair_in[p][...].reshape(own_rows[p], LANES).astype(f32)
        sums[p][...] = both.astype(bf16).reshape(sums[p].shape)
        for step in reversed(range(1, chips)):
            c_out(p, step).start()
        recv_c[p][chip] = sums[p][chip]

    for p, size in enumerate(PARTS):
        for k in range(size):
            c = starts[p] + k
            res = begun[c] + product(c, left, rows)
            for b in range(blocks):
                part[p][pl.ds(k * blocks + b, n, stride=size * blocks), :] = res[:, b * LANES : (b + 1) * LANES]
        pair_out[p][...] = part[p][...].astype(bf16).reshape(pair_out[p].shape)
        pair_copy(p, 1 - core).start()
        if p > 0:
            finish(p - 1)
    finish(len(PARTS) - 1)

    for p, size in enumerate(PARTS):
        c_all(p, recv_c[p]).wait_recv()
        total = recv_c[p][0].astype(f32)
        for h in range(1, chips):
            total = total + recv_c[p][h].astype(f32)
        for r in range(size * blocks):
            at = (starts[p] * blocks + r) * LANES
            cols = slice(at, at + LANES)
            out_ref[:, cols] = (total[r : r + 1, :] * ds[:, cols]).astype(out_ref.dtype)

    for p in range(PIECES):
        tok_all(p).wait_send()
        forward(p, core).wait_send()
    for j, (at, width) in enumerate(spans):
        x_send(j, width).wait_send()
    for o in range(owners):

        @pl.when(me != owner_at(o))
        def _():
            z_out(o).wait_send()

    def drain(count):
        every = rbuf.at[pl.ds(0, n - 1), pl.ds(0, count)]
        remote(every, every, r_ssem.at[0], r_rsem.at[0], partner).wait_send()

    by_count(drain)
    for p in range(len(PARTS)):
        pair_copy(p, 1 - core).wait_send()
        c_all(p, sums[p]).wait_send()


def fused(n, groups, tokens, gate_codes, gate_scales, up_codes, up_scales, down_codes, down_scales, hadamard):
    depth, units = gate_codes.shape
    width = down_codes.shape[1]
    tiles = units // LANES
    piece_rows = depth // (groups * PIECES * LANES)
    half_scales = (gate_scales.shape[0] // groups, units)
    rows = DOWN_COLS // LANES
    owners = n // 2
    held = -(-tiles // owners)
    spans = -(-units // WIDE)
    chips = n // 2
    bf16, f32, f8 = jnp.bfloat16, jnp.float32, jnp.float8_e4m3fn
    dma = pltpu.SemaphoreType.DMA
    vmem = pltpu.VMEM
    return pl.pallas_call(
        functools.partial(kernel, n, groups),
        out_shape=jax.ShapeDtypeStruct((1, width), bf16),
        in_specs=[pl.BlockSpec(memory_space=pl.ANY)] * 8,
        out_specs=pl.BlockSpec(memory_space=pltpu.VMEM),
        scratch_shapes=[
            vmem((SLOTS, 2, CHUNK, units), bf16),
            vmem((2, depth // groups, units), f8),
            vmem((DOWN_SLOTS, units, DOWN_COLS), bf16),
            vmem((width // DOWN_COLS, units, DOWN_COLS), f8),
            vmem(half_scales, f32),
            vmem(half_scales, f32),
            vmem((1, width), f32),
            vmem(hadamard.shape, hadamard.dtype),
            vmem((LANES, LANES), f32),
            vmem((LANES, units), bf16),
            vmem((units, units), f8),
            vmem((1, depth), bf16),
            vmem((depth // LANES, LANES), f32),
            vmem((groups, PIECES, piece_rows, LANES), bf16),
            vmem((PIECES, 2, n, piece_rows, LANES), bf16),
            vmem((2 * n * piece_rows, LANES), f32),
            vmem((PIECES, piece_rows // 2, 4 * n, WIDE), bf16),
            vmem((2, 2 * n, units), f32),
            vmem((spans, 2, n, WIDE), bf16),
            vmem((spans, 2, n, WIDE), bf16),
            vmem((owners, held, n, LANES), bf16),
            vmem((n, held, n, LANES), bf16),
            vmem((n, held, n, LANES), bf16),
            vmem((owners, held, n, LANES), bf16),
            vmem((width // DOWN_COLS, n, DOWN_COLS), f32),
            tuple(vmem((n * size * rows, LANES), f32) for size in PARTS),
            tuple(vmem((n, size * rows, LANES), bf16) for size in PARTS),
            tuple(vmem((chips, size * rows, LANES), bf16) for size in PARTS),
            tuple(vmem((chips, size * rows, LANES), bf16) for size in PARTS),
            tuple(vmem((chips, size * rows, LANES), bf16) for size in PARTS),
            dma((SLOTS,)),
            dma((5,)),
            dma((DOWN_SLOTS,)),
            dma((PIECES,)),
            dma((PIECES,)),
            dma((PIECES,)),
            dma((PIECES,)),
            dma((spans,)),
            dma((spans,)),
            dma((owners,)),
            dma((1,)),
            dma((1,)),
            dma((owners,)),
            dma((len(PARTS),)),
            dma((len(PARTS),)),
            dma((len(PARTS),)),
            dma((len(PARTS),)),
        ],
        compiler_params=pltpu.CompilerParams(
            collective_id=0, has_side_effects=True, vmem_limit_bytes=67043328
        ),
    )(
        tokens, gate_codes, gate_scales, up_codes, up_scales, down_codes, down_scales.reshape(1, width), hadamard,
    )


def fits(n, groups, tokens, gate_scales, down_codes):
    rows, depth = tokens.shape
    units, width = down_codes.shape
    scale_rows = gate_scales.shape[0]
    return (
        rows == 1
        and n == 16
        and groups == 2
        and HA % n == 0
        and units * n == HA * HB
        and HA // n <= LANES // 2
        and HB <= LANES // 2
        and HA // n % 8 == 0
        and 8 * HB % 32 == 0
        and depth == scale_rows * LANES
        and scale_rows % (groups * PIECES * 8) == 0
        and depth == 8 * groups * CHUNK
        and width == sum(PARTS) * DOWN_COLS
        and units % LANES == 0
        and n // 2 <= units // LANES <= n
    )


def per_device(
    tokens, gate_codes, gate_scales, up_codes, up_scales, down_codes, down_scales, hadamard
):
    n = lax.axis_size("hx")
    groups = lax.axis_size("groups")
    if fits(n, groups, tokens, gate_scales, down_codes):
        return fused(
            n, groups, tokens, gate_codes, gate_scales, up_codes, up_scales, down_codes, down_scales, hadamard
        )
    gate_weight = dequantize(gate_codes, gate_scales)
    up_weight = dequantize(up_codes, up_scales)
    tile_rows = lax.all_gather(tokens, "hx", axis=0, tiled=True)
    gate = jnp.dot(tile_rows, gate_weight, preferred_element_type=jnp.float32)
    up_part = jnp.dot(tile_rows, up_weight, preferred_element_type=jnp.float32)
    hidden = jax.nn.silu(gate) * up_part
    factor = hadamard.astype(jnp.float32)
    gathered = lax.all_to_all(
        hidden.astype(jnp.bfloat16), "hx", split_axis=0, concat_axis=1, tiled=True
    ).astype(hidden.dtype)
    row_count = gathered.shape[0]
    cube = gathered.reshape(row_count, HA, HB)
    cube = jnp.einsum("tab,ac->tcb", cube, sylvester(HA), precision=lax.Precision.HIGHEST)
    cube = jnp.einsum("tcb,bd->tcd", cube, factor, precision=lax.Precision.HIGHEST)
    turned = lax.all_to_all(
        cube.reshape(row_count, FF).astype(jnp.bfloat16),
        "hx",
        split_axis=1,
        concat_axis=0,
        tiled=True,
    ).astype(jnp.float32)
    rotated = (turned * (1.0 / math.sqrt(FF))).astype(jnp.bfloat16)
    summed = lax.psum_scatter(
        jnp.dot(rotated, down_codes, preferred_element_type=jnp.float32),
        "hx",
        scatter_dimension=0,
        tiled=True,
    )
    mixed = (summed * down_scales[None, :]).astype(jnp.bfloat16)
    return mixed


def solution(mesh):
    in_specs = (
        P(("groups", "hx"), None),
        P(None, "hx"),
        P(None, "hx"),
        P(None, "hx"),
        P(None, "hx"),
        P("hx", None),
        P(),
        P(),
    )
    out_specs = P(("groups", "hx"), None)
    return jax.shard_map(
        per_device, mesh=mesh, in_specs=in_specs, out_specs=out_specs, check_vma=False
    )
```

```python
import functools
import math

import jax
import jax.numpy as jnp
from jax import lax
from jax.experimental import pallas as pl
from jax.experimental.pallas import tpu as pltpu
from jax.sharding import PartitionSpec as P

HA = 512
HB = 52
FF = 26624


def sylvester(size):
    index_vec = jnp.arange(size, dtype=jnp.int32)
    parity = jnp.zeros((size, size), jnp.int32)
    for level in range(max(size.bit_length() - 1, 0)):
        left_bits = jnp.right_shift(index_vec[:, None], level) & 1
        right_bits = jnp.right_shift(index_vec[None, :], level) & 1
        parity = parity + left_bits * right_bits
    return (1 - 2 * (parity % 2)).astype(jnp.float32)


def dequantize(codes, scales):
    row_total, col_total = codes.shape
    group_total = scales.shape[0]
    grouped = codes.astype(jnp.float32).reshape(group_total, row_total // group_total, col_total)
    return (grouped * scales[:, None, :]).reshape(row_total, col_total).astype(jnp.bfloat16)


LANES = 128
WIDE = 2 * LANES
PIECES = 2
CHUNK = 512
SLOTS = 6
DOWN_COLS = 1024
DOWN_SLOTS = 3
BLOCK = 64
PARTS = (4, 4)


def kernel(
    n, groups, tok_ref, gate_ref, gscale_ref, up_ref, uscale_ref, down_ref, dscale_ref, had_ref,
    out_ref,
    ring, weights, dring, down, gs, us, ds, had, corner, table, local, tok_row, tok_f32, tok_out, tok, stage, lhs, acc,
    xsend, xrecv, zbuf, recv_z, rbuf, rot, begun, part, pair_out, pair_in, sums, recv_c,
    ring_sem, load_sem, down_sem, tok_ssem, tok_rsem, fwd_ssem, fwd_rsem, x_ssem, x_rsem, z_ssem, z_rsem, r_ssem, r_rsem,
    p_ssem, p_rsem, c_ssem, c_rsem,
):
    f32, bf16, f8 = jnp.float32, jnp.bfloat16, jnp.float8_e4m3fn
    mine = lax.axis_index("groups")
    me = lax.axis_index("hx")
    chips = n // 2
    chip, core = lax.div(me, 2), lax.rem(me, 2)
    units = gate_ref.shape[1]
    tiles = units // LANES
    half_rows = gate_ref.shape[0] // groups
    chunks = half_rows // CHUNK
    piece_rows = tok.shape[3]
    down_chunks = down.shape[0]
    other = lax.rem(mine + 1, groups)

    def device(group, index):
        return {"groups": group, "hx": index}

    def remote(src, dst, send_sem, recv_sem, peer):
        return pltpu.make_async_remote_copy(
            src_ref=src, dst_ref=dst, send_sem=send_sem, recv_sem=recv_sem,
            device_id=peer, device_id_type=pl.DeviceIdType.MESH,
        )

    def flip(index, mask):
        out = index
        for bit in range(mask.bit_length()):
            if mask >> bit & 1:
                out = out + (1 - 2 * lax.rem(lax.div(index, 1 << bit), 2)) * (1 << bit)
        return out

    def chip_at(step):
        return flip(chip, step)

    partner = device(mine, chip * 2 + 1 - core)
    peers = [device(mine, lax.rem(me + step, n)) for step in range(1, n)]
    across = [device(other, chip_at(step) * 2 + core) for step in range(chips)]

    def start_weights(c, slot):
        rows = pl.ds(pl.multiple_of(mine * half_rows + c * CHUNK, CHUNK), CHUNK)
        for w, src in enumerate((gate_ref, up_ref)):
            pltpu.make_async_copy(src.at[rows], ring.at[slot, w], ring_sem.at[slot]).start()

    def wait_weights(slot):
        pltpu.make_async_copy(ring.at[slot], ring.at[slot], ring_sem.at[slot]).wait()

    def down_copy(c):
        cols = pl.ds(c * DOWN_COLS, DOWN_COLS)
        return pltpu.make_async_copy(down_ref.at[:, cols], dring.at[c % DOWN_SLOTS], down_sem.at[c % DOWN_SLOTS])

    scale_rows = gs.shape[0]
    half_scales = pl.ds(pl.multiple_of(mine * scale_rows, scale_rows), scale_rows)
    loads = [
        pltpu.make_async_copy(src, dst, load_sem.at[i])
        for i, (src, dst) in enumerate(
            (
                (tok_ref, tok_row), (had_ref, had), (dscale_ref, ds),
                (gscale_ref.at[half_scales], gs), (uscale_ref.at[half_scales], us),
            )
        )
    ]

    barrier = pltpu.get_barrier_semaphore()
    for peer in peers + across:
        pl.semaphore_signal(barrier, inc=1, device_id=peer, device_id_type=pl.DeviceIdType.MESH)
    for copy in loads:
        copy.start()

    def first(c, carry):
        start_weights(c, c)
        return carry

    lax.fori_loop(0, SLOTS, first, 0)
    loads[0].wait()
    row = tok_row[...].astype(f32)
    for k in range(tok_f32.shape[0]):
        tok_f32[k : k + 1, :] = row[:, k * LANES : (k + 1) * LANES]
    for h in range(groups):
        for p in range(PIECES):
            start = (h * PIECES + p) * piece_rows
            tok_out[h, p] = tok_f32[start : start + piece_rows, :].astype(bf16)
    for p in range(PIECES):
        tok[p, core, chip] = tok_out[mine, p]
    loads[1].wait()

    half = LANES // 2
    hb = had.shape[0]
    ha = units // hb
    corner[...] = jnp.zeros_like(corner)
    corner[:hb, :hb] = had[...].astype(f32)
    left_bits = lax.broadcasted_iota(jnp.int32, (ha, ha), 0) & lax.broadcasted_iota(jnp.int32, (ha, ha), 1)
    parity = jnp.zeros((ha, ha), jnp.int32)
    for level in range(ha.bit_length() - 1):
        parity = parity ^ (jnp.right_shift(left_bits, level) & 1)
    corner[half : half + ha, half : half + ha] = (1 - 2 * parity).astype(f32)

    def digits(unit):
        high = jnp.floor((unit + 0.5) * (1.0 / hb))
        return high, unit - hb * high

    at = lax.broadcasted_iota(jnp.int32, (LANES, LANES), 0).astype(f32)
    unit = lax.broadcasted_iota(jnp.int32, (LANES, LANES), 1).astype(f32)
    parts = corner[...].astype(bf16)
    for i in range(tiles):
        high, low = digits(unit + float(i * LANES))
        pick = jnp.where((at == low) | (at == high + half), 1.0, 0.0).astype(bf16)
        table[:, i * LANES : (i + 1) * LANES] = jnp.dot(parts, pick, preferred_element_type=f32).astype(bf16)
    factors = table[...]

    def build(i, carry):
        shape = (LANES, LANES)
        unit = (lax.broadcasted_iota(jnp.int32, shape, 0) + i * LANES).astype(f32)
        at = lax.broadcasted_iota(jnp.int32, shape, 1).astype(f32)
        high, low = digits(unit)
        pick = jnp.concatenate(
            [jnp.where(at == low, 1.0, 0.0), jnp.where(at == high + half, 1.0, 0.0)], axis=0
        ).astype(bf16)
        both = jnp.dot(pick, factors, preferred_element_type=f32)
        rows = pl.ds(pl.multiple_of(i * LANES, LANES), LANES)
        local[rows, :] = (both[:LANES] * both[LANES:]).astype(f8)
        return carry

    octet = 8 * hb
    lax.fori_loop(0, -(-octet // LANES), build, 0)

    def signs(k, carry):
        rows = pl.ds(pl.multiple_of(k * 32, 32), 32)
        base = local[rows, :].astype(bf16)
        for i in range(1, ha // 8):
            to = pl.ds(pl.multiple_of(i * octet + k * 32, 32), 32)
            local[to, :] = (base * table[half + 8 * i : half + 8 * i + 1, :]).astype(f8)
        return carry

    pl.semaphore_wait(barrier, len(peers) + len(across))

    hops = [(d, step) for step in reversed(range(chips)) for d in reversed(range(groups)) if (d, step) != (0, 0)]

    def tok_send(p, d, step):
        group = lax.rem(mine + d, groups)
        return remote(
            tok_out.at[group, p], tok.at[p, core, d * chips + chip], tok_ssem.at[p], tok_rsem.at[p],
            device(group, chip_at(step) * 2 + core),
        )

    def tok_all(p):
        blocks = pl.ds(0, len(hops))
        at = tok.at[p, core, blocks]
        return remote(at, at, tok_ssem.at[p], tok_rsem.at[p], partner)

    def forward(p, which):
        return remote(tok.at[p, which], tok.at[p, which], fwd_ssem.at[p], fwd_rsem.at[p], partner)

    for p in range(PIECES):
        for d, step in hops:
            tok_send(p, d, step).start()

    lhs[...] = jnp.zeros_like(lhs)
    acc[...] = jnp.zeros_like(acc)
    lax.fori_loop(0, octet // 32, signs, 0)

    def convert(c):
        wait_weights(c % SLOTS)

        def block(k, carry):
            rows = pl.ds(pl.multiple_of(k * BLOCK, BLOCK), BLOCK)
            to = pl.ds(pl.multiple_of(c * CHUNK + k * BLOCK, BLOCK), BLOCK)
            for w in range(2):
                weights[w, to, :] = ring[c % SLOTS, w, rows, :].astype(f8)
            return carry

        lax.fori_loop(0, CHUNK // BLOCK, block, 0)
        if c + SLOTS < chunks:
            start_weights(c + SLOTS, c % SLOTS)
        elif c + SLOTS - chunks < DOWN_SLOTS:
            down_copy(c + SLOTS - chunks).start()

    def convert_down(c):
        down_copy(c).wait()

        def block(k, carry):
            rows = pl.ds(pl.multiple_of(k * BLOCK, BLOCK), BLOCK)
            down[c, rows, :] = dring[c % DOWN_SLOTS, rows, :].astype(f8)
            return carry

        lax.fori_loop(0, units // BLOCK, block, 0)
        if c + DOWN_SLOTS < down_chunks:
            down_copy(c + DOWN_SLOTS).start()

    def relay(p):
        tok_all(p).wait_recv()
        forward(p, core).start()

    def ready(p):
        forward(p, 1 - core).wait_recv()
        stage[...] = tok[p].reshape(stage.shape).astype(f32)
        for k in range(piece_rows):
            part_rows = [
                stage[pl.ds(w * n * piece_rows + k, n, stride=piece_rows), :] for w in range(2)
            ]
            both = jnp.concatenate(
                [part_rows[0][:chips], part_rows[1][:chips], part_rows[0][chips:], part_rows[1][chips:]], axis=0
            ).astype(bf16)
            q, odd = divmod(k, 2)
            lhs[p, q, odd * 2 * n : (odd + 1) * 2 * n, odd * LANES : (odd + 1) * LANES] = both

    def products(p, cols, tail):
        sums_now = [None, None]
        for q in range(piece_rows // 2):
            left = lhs[p, q]
            row = p * piece_rows + 2 * q
            rows = slice(row * LANES, (row + 2) * LANES)
            if tail:
                right = jnp.concatenate([weights[0, rows, cols], weights[1, rows, cols]], axis=1)
                scale = jnp.concatenate([gs[row : row + 2, cols], us[row : row + 2, cols]], axis=1)
                sides = [(right, scale)]
            else:
                sides = [(weights[w, rows, cols], scale[row : row + 2, cols]) for w, scale in ((0, gs), (1, us))]
            for w, (right, scale) in enumerate(sides):
                res = jnp.dot(left, right, preferred_element_type=f32)
                new = res[: 2 * n] * scale[0:1, :] + res[2 * n :] * scale[1:2, :]
                sums_now[w] = new if sums_now[w] is None else sums_now[w] + new
        if tail:
            width = sums_now[0].shape[1] // 2
            return sums_now[0][:, :width], sums_now[0][:, width:]
        return sums_now

    spans = [(at, min(WIDE, units - at)) for at in range(0, units, WIDE)]
    wide_tiles = WIDE // LANES

    def x_send(j, width):
        at = pl.ds(j * wide_tiles, width // LANES)
        return remote(xsend.at[at], xrecv.at[at], x_ssem.at[0], x_rsem.at[j], across[0])

    def run(pieces):
        final = pieces[-1] + 1 == PIECES
        for j, (at, width) in enumerate(spans):
            cols = slice(at, at + width)
            pair = None
            for p in pieces:
                new = products(p, cols, width < WIDE)
                pair = new if pair is None else [a + b for a, b in zip(pair, new)]
            for w in range(2):
                if not final:
                    acc[w, :, cols] += pair[w]
                else:
                    total = acc[w, :, cols] + pair[w]
                    acc[w, :n, cols] = total[:n]
                    for t in range(width // LANES):
                        xsend[j * wide_tiles + t, w] = total[n:, t * LANES : (t + 1) * LANES].astype(bf16)
            if final:
                x_send(j, width).start()

    for copy in loads[2:]:
        copy.wait()
    early = chunks // PIECES

    def convert_more():
        for c in range(early, SLOTS):
            convert(c)

    for c in range(early):
        convert(c)
    pl.when(me < 3 * n // 4)(convert_more)
    relay(0)
    relay(1)
    pl.when(me >= 3 * n // 4)(convert_more)
    ready(0)
    run([0])
    for c in range(SLOTS, chunks):
        convert(c)
    ready(1)
    run([1])

    for c in range(3):
        convert_down(c)
    turned = None
    for j, (at, width) in enumerate(spans):
        x_send(j, width).wait_recv()
        cols = slice(at, at + width)
        gate, lift = [
            acc[w, :n, cols]
            + jnp.concatenate([xrecv[j * wide_tiles + t, w] for t in range(width // LANES)], axis=1).astype(f32)
            for w in range(2)
        ]
        hidden = (gate / (1.0 + jnp.exp(-gate)) * lift).astype(bf16)
        new = jnp.dot(hidden, local[cols, :], preferred_element_type=f32)
        turned = new if turned is None else turned + new
    turned = turned.astype(bf16)

    owners = zbuf.shape[0]
    quarter = n // 4

    def owner_at(o):
        return quarter + (o % 2) * quarter + o // 2

    def held(o):
        return len(range(o, tiles, owners))

    for j in range(tiles):
        zbuf[j % owners, j // owners] = turned[:, j * LANES : (j + 1) * LANES]

    def z_out(o):
        count = pl.ds(0, held(o))
        return remote(
            zbuf.at[o, count], recv_z.at[me, count], z_ssem.at[o], z_rsem.at[0], device(mine, owner_at(o))
        )

    for o in range(owners):

        @pl.when(me != owner_at(o))
        def _():
            z_out(o).start()

        @pl.when(me == owner_at(o))
        def _():
            recv_z[me] = zbuf[o]

    for c in range(3, 6):
        convert_down(c)

    place = me - quarter
    number = lax.rem(place, quarter) * 2 + lax.div(place, quarter)
    owns = jnp.logical_and(me >= quarter, me < 3 * quarter)
    extra = tiles % owners
    scale = 1.0 / math.sqrt(units * n)

    def r_out(i, count):
        at = pl.ds(0, count)
        peer = flip(me, i)
        return remote(rbuf.at[peer, at], rot.at[number, at], r_ssem.at[0], r_rsem.at[number], device(mine, peer))

    def turn(count):
        at = pl.ds(0, count)
        every = recv_z.at[pl.ds(0, n - 1), at]
        remote(every, every, z_ssem.at[0], z_rsem.at[0], partner).wait_recv()
        for t in range(count):
            cube = [recv_z[h, t].astype(f32) for h in range(n)]
            span = 1
            while span < n:
                nxt = list(cube)
                for h in range(n):
                    if h & span == 0:
                        nxt[h] = cube[h] + cube[h | span]
                        nxt[h | span] = cube[h] - cube[h | span]
                cube = nxt
                span *= 2
            for h in range(n):
                rbuf[h, t] = (cube[h] * scale).astype(bf16)
        for i in reversed(range(1, n)):
            r_out(i, count).start()
        rot[number] = rbuf[me]

    many, few = held(0), held(owners - 1)

    def by_count(action):
        if extra == 0:
            pl.when(owns)(lambda: action(many))
        else:
            pl.when(jnp.logical_and(owns, number < extra))(lambda: action(many))
            pl.when(jnp.logical_and(owns, number >= extra))(lambda: action(few))

    by_count(turn)

    for c in range(6, down_chunks):
        convert_down(c)

    def arrived(parity):
        for o in range(parity, owners, 2):

            @pl.when(me != owner_at(o))
            def _(o=o):
                count = pl.ds(0, held(o))
                remote(
                    rbuf.at[0, count], rot.at[o, count], r_ssem.at[0], r_rsem.at[o], device(mine, owner_at(o))
                ).wait_recv()

    side = lax.div(me, n // 2)
    even = [(o, k) for k in range(rot.shape[1]) for o in range(0, owners, 2) if o + k * owners < tiles]
    common = [(o, k) for o, k in even if o + 1 + k * owners < tiles]
    single = [(o, k) for o, k in even if (o, k) not in common]

    def operands(parity, pairs):
        left = [rot[o + parity, k] for o, k in pairs]
        rows = [pl.ds(pl.multiple_of((o + k * owners + parity) * LANES, LANES), LANES) for o, k in pairs]
        return left, rows

    def product(c, left, rows):
        right = jnp.concatenate([down[c, at, :] for at in rows], axis=0)
        return jnp.dot(jnp.concatenate(left, axis=1), right, preferred_element_type=f32)

    pl.when(side == 0)(lambda: arrived(0))
    pl.when(side == 1)(lambda: arrived(1))
    left, rows = operands(side, common)
    for c in range(down_chunks):
        begun[c] = product(c, left, rows)
    pl.when(side == 0)(lambda: arrived(1))
    pl.when(side == 1)(lambda: arrived(0))
    left, rows = operands(1 - side, common)
    more, more_rows = operands(0, single)
    left, rows = left + more, rows + more_rows

    blocks = DOWN_COLS // LANES
    starts = [sum(PARTS[:p]) for p in range(len(PARTS))]
    own_rows = [chips * size * blocks for size in PARTS]

    def pair_copy(p, which):
        at = pl.ds(which * chips, chips)
        return remote(pair_out[p].at[at], pair_in[p], p_ssem.at[p], p_rsem.at[p], partner)

    def c_out(p, step):
        to = chip_at(step)
        return remote(
            sums[p].at[to], recv_c[p].at[chip], c_ssem.at[p], c_rsem.at[p], device(mine, to * 2 + core)
        )

    def c_all(p, ref):
        at = ref.at[pl.ds(0, chips - 1)]
        return remote(at, at, c_ssem.at[p], c_rsem.at[p], partner)

    def finish(p):
        pair_copy(p, core).wait_recv()
        rows = pl.ds(pl.multiple_of(core * own_rows[p], own_rows[p]), own_rows[p])
        both = part[p][rows, :] + pair_in[p][...].reshape(own_rows[p], LANES).astype(f32)
        sums[p][...] = both.astype(bf16).reshape(sums[p].shape)
        for step in reversed(range(1, chips)):
            c_out(p, step).start()
        recv_c[p][chip] = sums[p][chip]

    for p, size in enumerate(PARTS):
        for k in range(size):
            c = starts[p] + k
            res = begun[c] + product(c, left, rows)
            for b in range(blocks):
                part[p][pl.ds(k * blocks + b, n, stride=size * blocks), :] = res[:, b * LANES : (b + 1) * LANES]
        pair_out[p][...] = part[p][...].astype(bf16).reshape(pair_out[p].shape)
        pair_copy(p, 1 - core).start()
        if p > 0:
            finish(p - 1)
    finish(len(PARTS) - 1)

    for p, size in enumerate(PARTS):
        c_all(p, recv_c[p]).wait_recv()
        total = recv_c[p][0].astype(f32)
        for h in range(1, chips):
            total = total + recv_c[p][h].astype(f32)
        for r in range(size * blocks):
            at = (starts[p] * blocks + r) * LANES
            cols = slice(at, at + LANES)
            out_ref[:, cols] = (total[r : r + 1, :] * ds[:, cols]).astype(out_ref.dtype)

    for p in range(PIECES):
        tok_all(p).wait_send()
        forward(p, core).wait_send()
    remote(xsend, xrecv, x_ssem.at[0], x_rsem.at[0], across[0]).wait_send()
    for o in range(owners):

        @pl.when(me != owner_at(o))
        def _():
            z_out(o).wait_send()

    def drain(count):
        every = rbuf.at[pl.ds(0, n - 1), pl.ds(0, count)]
        remote(every, every, r_ssem.at[0], r_rsem.at[0], partner).wait_send()

    by_count(drain)
    for p in range(len(PARTS)):
        pair_copy(p, 1 - core).wait_send()
        c_all(p, sums[p]).wait_send()


def fused(n, groups, tokens, gate_codes, gate_scales, up_codes, up_scales, down_codes, down_scales, hadamard):
    depth, units = gate_codes.shape
    width = down_codes.shape[1]
    tiles = units // LANES
    piece_rows = depth // (groups * PIECES * LANES)
    half_scales = (gate_scales.shape[0] // groups, units)
    rows = DOWN_COLS // LANES
    owners = n // 2
    held = -(-tiles // owners)
    spans = -(-units // WIDE)
    chips = n // 2
    bf16, f32, f8 = jnp.bfloat16, jnp.float32, jnp.float8_e4m3fn
    dma = pltpu.SemaphoreType.DMA
    vmem = pltpu.VMEM
    return pl.pallas_call(
        functools.partial(kernel, n, groups),
        out_shape=jax.ShapeDtypeStruct((1, width), bf16),
        in_specs=[pl.BlockSpec(memory_space=pl.ANY)] * 8,
        out_specs=pl.BlockSpec(memory_space=pltpu.VMEM),
        scratch_shapes=[
            vmem((SLOTS, 2, CHUNK, units), bf16),
            vmem((2, depth // groups, units), f8),
            vmem((DOWN_SLOTS, units, DOWN_COLS), bf16),
            vmem((width // DOWN_COLS, units, DOWN_COLS), f8),
            vmem(half_scales, f32),
            vmem(half_scales, f32),
            vmem((1, width), f32),
            vmem(hadamard.shape, hadamard.dtype),
            vmem((LANES, LANES), f32),
            vmem((LANES, units), bf16),
            vmem((units, units), f8),
            vmem((1, depth), bf16),
            vmem((depth // LANES, LANES), f32),
            vmem((groups, PIECES, piece_rows, LANES), bf16),
            vmem((PIECES, 2, n, piece_rows, LANES), bf16),
            vmem((2 * n * piece_rows, LANES), f32),
            vmem((PIECES, piece_rows // 2, 4 * n, WIDE), bf16),
            vmem((2, 2 * n, units), f32),
            vmem((tiles, 2, n, LANES), bf16),
            vmem((tiles, 2, n, LANES), bf16),
            vmem((owners, held, n, LANES), bf16),
            vmem((n, held, n, LANES), bf16),
            vmem((n, held, n, LANES), bf16),
            vmem((owners, held, n, LANES), bf16),
            vmem((width // DOWN_COLS, n, DOWN_COLS), f32),
            tuple(vmem((n * size * rows, LANES), f32) for size in PARTS),
            tuple(vmem((n, size * rows, LANES), bf16) for size in PARTS),
            tuple(vmem((chips, size * rows, LANES), bf16) for size in PARTS),
            tuple(vmem((chips, size * rows, LANES), bf16) for size in PARTS),
            tuple(vmem((chips, size * rows, LANES), bf16) for size in PARTS),
            dma((SLOTS,)),
            dma((5,)),
            dma((DOWN_SLOTS,)),
            dma((PIECES,)),
            dma((PIECES,)),
            dma((PIECES,)),
            dma((PIECES,)),
            dma((1,)),
            dma((spans,)),
            dma((owners,)),
            dma((1,)),
            dma((1,)),
            dma((owners,)),
            dma((len(PARTS),)),
            dma((len(PARTS),)),
            dma((len(PARTS),)),
            dma((len(PARTS),)),
        ],
        compiler_params=pltpu.CompilerParams(
            collective_id=0, has_side_effects=True, vmem_limit_bytes=67043328
        ),
    )(
        tokens, gate_codes, gate_scales, up_codes, up_scales, down_codes, down_scales.reshape(1, width), hadamard,
    )


def fits(n, groups, tokens, gate_scales, down_codes):
    rows, depth = tokens.shape
    units, width = down_codes.shape
    scale_rows = gate_scales.shape[0]
    return (
        rows == 1
        and n == 16
        and groups == 2
        and HA % n == 0
        and units * n == HA * HB
        and HA // n <= LANES // 2
        and HB <= LANES // 2
        and HA // n % 8 == 0
        and 8 * HB % 32 == 0
        and depth == scale_rows * LANES
        and scale_rows % (groups * PIECES * 8) == 0
        and depth == 8 * groups * CHUNK
        and width == sum(PARTS) * DOWN_COLS
        and units % LANES == 0
        and n // 2 <= units // LANES <= n
    )


def per_device(
    tokens, gate_codes, gate_scales, up_codes, up_scales, down_codes, down_scales, hadamard
):
    n = lax.axis_size("hx")
    groups = lax.axis_size("groups")
    if fits(n, groups, tokens, gate_scales, down_codes):
        return fused(
            n, groups, tokens, gate_codes, gate_scales, up_codes, up_scales, down_codes, down_scales, hadamard
        )
    gate_weight = dequantize(gate_codes, gate_scales)
    up_weight = dequantize(up_codes, up_scales)
    tile_rows = lax.all_gather(tokens, "hx", axis=0, tiled=True)
    gate = jnp.dot(tile_rows, gate_weight, preferred_element_type=jnp.float32)
    up_part = jnp.dot(tile_rows, up_weight, preferred_element_type=jnp.float32)
    hidden = jax.nn.silu(gate) * up_part
    factor = hadamard.astype(jnp.float32)
    gathered = lax.all_to_all(
        hidden.astype(jnp.bfloat16), "hx", split_axis=0, concat_axis=1, tiled=True
    ).astype(hidden.dtype)
    row_count = gathered.shape[0]
    cube = gathered.reshape(row_count, HA, HB)
    cube = jnp.einsum("tab,ac->tcb", cube, sylvester(HA), precision=lax.Precision.HIGHEST)
    cube = jnp.einsum("tcb,bd->tcd", cube, factor, precision=lax.Precision.HIGHEST)
    turned = lax.all_to_all(
        cube.reshape(row_count, FF).astype(jnp.bfloat16),
        "hx",
        split_axis=1,
        concat_axis=0,
        tiled=True,
    ).astype(jnp.float32)
    rotated = (turned * (1.0 / math.sqrt(FF))).astype(jnp.bfloat16)
    summed = lax.psum_scatter(
        jnp.dot(rotated, down_codes, preferred_element_type=jnp.float32),
        "hx",
        scatter_dimension=0,
        tiled=True,
    )
    mixed = (summed * down_scales[None, :]).astype(jnp.bfloat16)
    return mixed


def solution(mesh):
    in_specs = (
        P(("groups", "hx"), None),
        P(None, "hx"),
        P(None, "hx"),
        P(None, "hx"),
        P(None, "hx"),
        P("hx", None),
        P(),
        P(),
    )
    out_specs = P(("groups", "hx"), None)
    return jax.shard_map(
        per_device, mesh=mesh, in_specs=in_specs, out_specs=out_specs, check_vma=False
    )
```
